256 devices in a mesh: dom: 32 (over y, x, core), blk: 8 (over z).
Axes of the slice: x: 4, y: 4, z: 8, core: 2. Of those that a mesh axis runs over, the one named last changes fastest.
Arguments:
- displacement: float32 [3, 256, 64, 128], P(None, 'dom', 'blk'), may hold values from -6 to 6
- velocity: float32 [3, 256, 64, 128], P(None, 'dom', 'blk'), may hold values from -6 to 6
- load: float32 [3, 256, 64, 128], P(None, 'dom', 'blk'), may hold values from -6 to 6
- density: float32 [256, 64, 128], P('dom', 'blk'), may hold values from 0.5 to 1.5
- block_class: int32 [32, 8, 16], P('dom', 'blk'), may hold values from 0 to 2
- host_element: int32 [8, 131072], P('blk', 'dom'), may hold values from 0 to 7038, as said below
- host_coords: float32 [3, 8, 131072], P(None, 'blk', 'dom'), may hold values from 0 to 1
- fibre_slot: int32 [512, 8, 128], P('dom', 'blk'), may hold values from 0 to 4095, as said below
- fibre_angles: float32 [2, 512, 8, 128], P(None, 'dom', 'blk'), may hold values from -3.140625 to 3.140625
- fibre_stiffness: float32 [512, 8], P('dom', 'blk'), may hold values from 0.5 to 4
Outputs:
- new_displacement: float32 [3, 256, 64, 128], P(None, 'dom', 'blk')
- new_velocity: float32 [3, 256, 64, 128], P(None, 'dom', 'blk')
The draws below stay inside these ranges and needn't reach their ends.
Inputs may be any that keep to these rules, and one draw needn't show every extreme that they name: `host_element`: each entry is (i * 8 + j) * 128 + k with i < 7, j < 7, k < 127, a voxel element of the device's own block; a device's entries are laid out as 128 slots for each owner index along dom, in order. `fibre_slot`: the entries of one device are distinct; value // 128 is the dom index of the host device in the same blk column and value % 128 the slot among that host's 128 slots for this owner; on every device all 128 slots of one host are used.
All inputs are finite; a program needn't handle non-finite values.
Results may differ from the reference program's by a relative error of at most 0.0003.
Values sent between devices are 32-bit elements; how exact they have to be, the bound alone decides.
No kernel may reach another device: no remote copies, remote signals or barrier semaphores. Data moves between devices by JAX's collectives and lax.ppermute only.
A program may use at most 64 MiB of HBM per device.

```python
import math
import jax
import jax.numpy as jnp
import numpy as np
from jax import lax

CX = 8
CY = 8
CZ = 128
FIB_DEV = 16
FNODES = 128
SLOTS = 4096
CAP = 128
NX = 256
NY = 64
FIB_ROWS = 512
N_DOM = 32
N_BLK = 8


def draw_host_element(key, part):
    key_x, key_y, key_z = jax.random.split(jax.random.fold_in(key, 7), 3)
    shape = (N_BLK, N_DOM * SLOTS)
    along_x = jax.random.randint(key_x, shape, 0, CX - 1)
    along_y = jax.random.randint(key_y, shape, 0, CY - 1)
    along_z = jax.random.randint(key_z, shape, 0, CZ - 1)
    flat = (along_x * CY + along_y) * CZ + along_z
    highest = ((CX - 2) * CY + (CY - 2)) * CZ + (CZ - 2)
    blocks = flat.reshape(N_BLK, N_DOM, SLOTS)
    blocks = blocks.at[:, :, 0].set(highest).at[:, :, 1].set(0)
    return blocks.reshape(shape).astype(jnp.int32)


def draw_fibre_slot(key, part):
    count = FIB_DEV * FNODES

    def single(sub):
        key_order, key_host, key_mix = jax.random.split(sub, 3)
        order = jax.random.permutation(key_order, SLOTS).astype(jnp.int32)
        chosen = jax.random.randint(key_host, (), 0, N_DOM)
        owner_block = jnp.arange(SLOTS, dtype=jnp.int32) // CAP
        priority = order + jnp.where(owner_block == chosen, SLOTS, 0).astype(jnp.int32)
        picked = lax.top_k(priority, count)[1].astype(jnp.int32)
        mixing = jax.random.permutation(key_mix, count)
        return picked[mixing]
    subs = jax.random.split(jax.random.fold_in(key, 11), N_DOM * N_BLK)
    table = jax.vmap(single)(subs)
    table = table.reshape(N_DOM, N_BLK, FIB_DEV, FNODES).transpose(0, 2, 1, 3)
    return table.reshape(N_DOM * FIB_DEV, N_BLK, FNODES).astype(jnp.int32)


def plant(drawn, own_key, smallest, top_value):
    longest = drawn.shape.index(max(drawn.shape))
    spots = []
    for shift in (0, 1):
        where = [jax.random.randint(jax.random.fold_in(own_key, axis), (), 0, length) for axis, length in enumerate(drawn.shape)]
        where[longest] = (where[longest] + shift) % drawn.shape[longest]
        spots.append(tuple(where))
    return drawn.at[spots[0]].set(smallest).at[spots[1]].set(top_value)


def levels(stream_key, extent, pieces, low, high):
    loudness, own = 1.0, jax.random.fold_in(stream_key, 6)
    for axis_at, parts in pieces:
        heights = jnp.exp(jax.random.uniform(jax.random.fold_in(own, axis_at), (parts,), jnp.float32, low / len(pieces), high / len(pieces)))
        loudness = loudness * jnp.repeat(heights, extent[axis_at] // parts).reshape([-1 if axis == axis_at else 1 for axis in range(len(extent))])
    return loudness


def normal_values(own_key, shape, scale, limit, shards=(), held_as=jnp.bfloat16):
    values = jax.random.normal(own_key, shape, jnp.float32) * scale
    if len(shards) > 0:
        values = levels(own_key, shape, shards, -0.22, 0.18) * values
    return jnp.clip(values, min=-limit, max=limit).astype(held_as)


def setup_inputs(seed: int = 0) -> dict:
    splits = jax.random.split(jax.random.key(seed), 11)
    displacement = normal_values(splits[0], (3, NX, NY, CZ), 1.0, 6.0, ((1, 32), (2, 8)), jnp.float32)
    velocity = normal_values(splits[1], (3, NX, NY, CZ), 1.0, 6.0, ((1, 32), (2, 8)), jnp.float32)
    load = normal_values(splits[2], (3, NX, NY, CZ), 1.0, 6.0, ((1, 32), (2, 8)), jnp.float32)
    density = jnp.clip(jnp.exp(math.log(1.5) - 1.0986123 * jax.random.uniform(splits[3], (NX, NY, CZ), jnp.float32) ** levels(splits[3], (NX, NY, CZ), ((0, 32), (1, 8)), -0.2, 0.2)), 0.5, 1.5)
    block_class = plant(jax.random.randint(splits[4], (NX // 8, NY // 8, CZ // 8), 0, 3), jax.random.fold_in(splits[4], 1), 0, 2).astype(jnp.int32)
    host_element = draw_host_element(jax.random.fold_in(splits[10], 71), 0)
    host_coords = jnp.clip(1.0 * jax.random.uniform(splits[6], (3, N_BLK, N_DOM * SLOTS), jnp.float32) ** levels(splits[6], (3, N_BLK, N_DOM * SLOTS), ((1, 8), (2, 32)), -0.2, 0.2), 0.0, 1.0)
    fibre_slot = draw_fibre_slot(jax.random.fold_in(splits[10], 71), 0)
    fibre_angles = jnp.clip(jax.random.uniform(splits[8], (2, FIB_ROWS, N_BLK, FNODES), jnp.float32, -3.140625, 3.140625), -3.140625, 3.140625)
    fibre_stiffness = jnp.clip(jnp.exp(math.log(4.0) - 2.0794415 * jax.random.uniform(splits[9], (FIB_ROWS, N_BLK), jnp.float32) ** levels(splits[9], (FIB_ROWS, N_BLK), ((0, 32), (1, 8)), -0.2, 0.2)), 0.5, 4.0)
    return {"displacement": displacement, "velocity": velocity, "load": load, "density": density, "block_class": block_class, "host_element": host_element, "host_coords": host_coords, "fibre_slot": fibre_slot, "fibre_angles": fibre_angles, "fibre_stiffness": fibre_stiffness}


class_values = (1.0, 0.45, 0.12)
time_step = 0.25
damping = 0.5

def stiffness_table():
    poisson = 0.3
    lame = poisson / ((1 + poisson) * (1 - 2 * poisson))
    shear = 0.5 / (1 + poisson)
    elastic = np.zeros((6, 6))
    elastic[:3, :3] = lame
    for place in range(3):
        elastic[place, place] += 2 * shear
        elastic[place + 3, place + 3] = shear
    points = [0.5 - 0.5 / np.sqrt(3.0), 0.5 + 0.5 / np.sqrt(3.0)]
    table = np.zeros((24, 24))
    for gauss_r in points:
        for gauss_p in points:
            for gauss_q in points:
                strain = np.zeros((6, 24))
                for corner in range(8):
                    x_bit, y_bit, z_bit = (corner // 4, corner // 2 % 2, corner % 2)
                    along_r = gauss_r if x_bit else 1 - gauss_r
                    along_p = gauss_p if y_bit else 1 - gauss_p
                    along_q = gauss_q if z_bit else 1 - gauss_q
                    d_x = (2 * x_bit - 1) * along_p * along_q
                    d_y = along_r * (2 * y_bit - 1) * along_q
                    d_z = along_r * along_p * (2 * z_bit - 1)
                    column = 3 * corner
                    strain[0, column] = d_x
                    strain[1, column + 1] = d_y
                    strain[2, column + 2] = d_z
                    strain[3, column] = d_y
                    strain[3, column + 1] = d_x
                    strain[4, column + 1] = d_z
                    strain[4, column + 2] = d_y
                    strain[5, column] = d_z
                    strain[5, column + 2] = d_x
                table += 0.125 * strain.T @ elastic @ strain
    return table

def class_moduli(block_class):
    factor = jnp.zeros(block_class.shape, jnp.float32)
    for index, value in enumerate(class_values):
        factor = factor + jnp.where(block_class == index, jnp.float32(value), jnp.float32(0.0))
    bx, by, bz = block_class.shape
    wide = jnp.broadcast_to(factor[:, None, :, None, :, None], (bx, 8, by, 8, bz, 8))
    return wide.reshape(bx * 8, by * 8, bz * 8)

def lift_depth(local):
    return jnp.concatenate([local[..., 1:], jnp.zeros_like(local[..., :1])], axis=-1)

def element_forces(padded, moduli, density):
    width = padded.shape[1] - 2
    height = padded.shape[2] - 2
    depth = padded.shape[3]
    table = jnp.asarray(stiffness_table(), jnp.float32)
    element = jnp.zeros((24, width + 1, height + 1, depth), jnp.float32)
    for corner in range(8):
        x_bit, y_bit, z_bit = (corner // 4, corner // 2 % 2, corner % 2)
        local = padded[:, x_bit:x_bit + width + 1, y_bit:y_bit + height + 1, :]
        if z_bit:
            local = lift_depth(local)
        element = element + jnp.einsum('ij,jxyz->ixyz', table[:, 3 * corner:3 * corner + 3], local, precision=lax.Precision.HIGHEST)
    element = element * moduli[None, :width + 1, :height + 1, :]
    weight = density[:width + 1, :height + 1, :]
    force = jnp.zeros((3, width, height, depth), jnp.float32)
    mass = jnp.zeros((width, height, depth), jnp.float32)
    for corner in range(8):
        x_bit, y_bit, z_bit = (corner // 4, corner // 2 % 2, corner % 2)
        piece = element[3 * corner:3 * corner + 3, 1 - x_bit:1 - x_bit + width, 1 - y_bit:1 - y_bit + height, :]
        share = weight[1 - x_bit:1 - x_bit + width, 1 - y_bit:1 - y_bit + height, :]
        if z_bit:
            piece = jnp.pad(piece[..., :-1], ((0, 0), (0, 0), (0, 0), (1, 0)))
            share = jnp.pad(share[..., :-1], ((0, 0), (0, 0), (1, 0)))
        force = force + piece
        mass = mass + 0.125 * share
    return (force, mass)

def corner_table(element, coords, height, depth):
    rows = []
    weights = []
    for corner in range(8):
        x_bit, y_bit, z_bit = (corner // 4, corner // 2 % 2, corner % 2)
        rows.append(element + (x_bit * height * depth + y_bit * depth + z_bit))
        along_r = coords[0] if x_bit else 1.0 - coords[0]
        along_p = coords[1] if y_bit else 1.0 - coords[1]
        along_q = coords[2] if z_bit else 1.0 - coords[2]
        weights.append(along_r * along_p * along_q)
    return (jnp.stack(rows).astype(jnp.int32), jnp.stack(weights))

def interpolate(field, element, coords, height, depth):
    indices, weights = corner_table(element, coords, height, depth)
    gathered = field[:, indices]
    return lax.optimization_barrier(jnp.sum(gathered * weights[None], axis=1))

def spread(force, element, coords, count, height, depth):
    indices, weights = corner_table(element, coords, height, depth)
    terms = force[:, None, :] * weights[None]
    return jnp.zeros((3, count), jnp.float32).at[:, indices].add(terms)

def fibre_forces(places, slots, angles, stiffness):
    node = places[:, slots]
    direction = jnp.stack([jnp.cos(angles[0]) * jnp.cos(angles[1]), jnp.sin(angles[0]) * jnp.cos(angles[1]), jnp.sin(angles[1])])
    ahead = jnp.concatenate([node[..., 1:], node[..., -1:]], axis=-1)
    strain = lax.optimization_barrier(jnp.sum(direction * (ahead - node), axis=0))
    live = lax.broadcasted_iota(jnp.int32, strain.shape, 1) < strain.shape[1] - 1
    tension = jnp.where(live, stiffness * jnp.maximum(strain, 0.0), jnp.float32(0.0))
    pull = tension[None] * direction
    behind = jnp.concatenate([jnp.zeros_like(pull[..., :1]), pull[..., :-1]], axis=-1)
    return jnp.zeros(places.shape, jnp.float32).at[:, slots].set(pull - behind)

def reference(displacement, velocity, load, density, block_class, host_element, host_coords, fibre_slot, fibre_angles, fibre_stiffness):
    moduli = class_moduli(block_class) * density * density
    padded_field = jnp.pad(displacement, ((0, 0), (1, 1), (1, 1), (0, 0)))
    padded_moduli = jnp.pad(moduli, ((1, 1), (1, 1), (0, 0)))
    padded_density = jnp.pad(density, ((1, 1), (1, 1), (0, 0)))

    def slab(start):
        return element_forces(lax.dynamic_slice_in_dim(padded_field, start, CX + 2, 1), lax.dynamic_slice_in_dim(padded_moduli, start, CX + 2, 0), lax.dynamic_slice_in_dim(padded_density, start, CX + 2, 0))
    starts = jnp.arange(N_DOM, dtype=jnp.int32) * CX
    slab_force, slab_mass = lax.map(slab, starts)
    elastic = slab_force.transpose(1, 0, 2, 3, 4).reshape(3, NX, NY, CZ)
    mass = slab_mass.reshape(NX, NY, CZ)
    count = N_DOM * N_BLK
    blocks = displacement.reshape(3, N_DOM, CX, N_BLK, CY, CZ).transpose(1, 3, 0, 2, 4, 5).reshape(count, 3, CX * CY * CZ)
    elements = host_element.reshape(N_BLK, N_DOM, SLOTS).transpose(1, 0, 2).reshape(count, SLOTS)
    coords = host_coords.reshape(3, N_BLK, N_DOM, SLOTS).transpose(2, 1, 0, 3).reshape(count, 3, SLOTS)

    def host_places(item):
        return interpolate(item[0], item[1], item[2], CY, CZ)
    places = lax.map(host_places, (blocks, elements, coords))
    owned = places.reshape(N_DOM, N_BLK, 3, N_DOM, CAP).transpose(3, 1, 2, 0, 4).reshape(count, 3, SLOTS)
    slots = fibre_slot.reshape(N_DOM, FIB_DEV, N_BLK, FNODES).transpose(0, 2, 1, 3).reshape(count, FIB_DEV, FNODES)
    angles = fibre_angles.reshape(2, N_DOM, FIB_DEV, N_BLK, FNODES).transpose(1, 3, 0, 2, 4).reshape(count, 2, FIB_DEV, FNODES)
    stiffness = fibre_stiffness.reshape(N_DOM, FIB_DEV, N_BLK).transpose(0, 2, 1).reshape(count, FIB_DEV, 1)
    pulls = jax.vmap(fibre_forces)(owned, slots, angles, stiffness)
    hosted = pulls.reshape(N_DOM, N_BLK, 3, N_DOM, CAP).transpose(3, 1, 2, 0, 4).reshape(count, 3, SLOTS)

    def host_spread(item):
        return spread(item[0], item[1], item[2], CX * CY * CZ, CY, CZ)
    spreads = lax.map(host_spread, (hosted, elements, coords))
    fibre = spreads.reshape(N_DOM, N_BLK, 3, CX, CY, CZ).transpose(2, 0, 3, 1, 4, 5).reshape(3, NX, NY, CZ)
    acceleration = (load - elastic + fibre) / mass[None] - damping * velocity
    new_velocity = velocity + time_step * acceleration
    new_displacement = displacement + time_step * new_velocity
    return (new_displacement, new_velocity)
```

```python
import jax
import jax.numpy as jnp
from jax import lax
from jax.experimental import pallas as pl
from jax.experimental.pallas import tpu as pltpu
from jax.sharding import Mesh
from jax.sharding import PartitionSpec as P

DOM = ("dom_0", "dom_1", "dom_2")
CLASS_VALUES = (1.0, 0.45, 0.12)
TIME_STEP = 0.25
DAMPING = 0.5
LAME = 0.3 / (1.3 * 0.4)
SHEAR = 0.5 / 1.3

F32 = jnp.float32
BF16 = jnp.bfloat16
LANES = 128
ROWS = 104
ROWS_PAD = 120


def sds(shape, dtype=F32):
    return jax.ShapeDtypeStruct(shape, dtype)


def split(value):
    high = value.astype(BF16)
    low = (value - high.astype(F32)).astype(BF16)
    return high, low


def iota(shape, axis):
    return lax.broadcasted_iota(jnp.int32, shape, axis)


def hat(lowest, along, count):
    where = iota((count, LANES), 0)
    return jnp.where(
        where == lowest, 1.0 - along, jnp.where(where == lowest + 1, along, 0.0)
    )


def planar_weights(element, along_r, along_p):
    weight_x = hat(element >> 10, along_r, 8)
    weight_y = hat((element >> 7) & 7, along_p, 8)
    return (weight_x[:, None, :] * weight_y[None]).reshape(64, LANES)


def interpolate_kernel(
    odd_ref, u_ref, element_ref, coords_ref, density_ref, class_ref,
    places_ref, high_ref, low_ref, modulus_ref, even_ref, odd_swap_ref,
):
    lane_block = iota((16, LANES), 1) >> 3
    pick = (lane_block == iota((16, LANES), 0)).astype(F32)
    kind = jnp.dot(
        jnp.broadcast_to(class_ref[...].astype(F32), (8, 16)), pick, preferred_element_type=F32
    )
    factor = jnp.zeros((8, LANES), F32)
    for index, value in enumerate(CLASS_VALUES):
        factor = factor + jnp.where(kind == float(index), value, 0.0)
    density = density_ref[...]
    modulus = factor[None] * density * density
    modulus_ref[...] = modulus
    odd = odd_ref[0, 0] != 0
    for comp in range(5):
        if comp < 3:
            first, last = u_ref[comp, 0], u_ref[comp, 7]
        else:
            source = modulus if comp == 3 else density
            first, last = source[0], source[7]
        even_ref[comp] = jnp.where(odd, first, last)
        odd_swap_ref[comp] = jnp.where(odd, last, first)

    field_high, field_low = split(u_ref[...].reshape(192, LANES))
    field = jnp.concatenate([field_high, field_low], axis=1)
    for pair in range(16):
        highs, lows = [], []
        for half in range(2):
            owner = 2 * pair + half
            element = element_ref[pl.ds(owner, 1), :]
            weight_z = hat(element & 127, coords_ref[2, pl.ds(owner, 1), :], LANES)
            high, low = split(weight_z)
            high_ref[owner] = high
            low_ref[owner] = low
            highs.append(high)
            lows.append(low)
        high = jnp.concatenate(highs, axis=1)
        low = jnp.concatenate(lows, axis=1)
        sums = jnp.dot(
            field, jnp.concatenate([high, high], axis=0), preferred_element_type=F32
        ) + jnp.dot(field_high, low, preferred_element_type=F32)
        for half in range(2):
            owner = 2 * pair + half
            planar = planar_weights(
                element_ref[pl.ds(owner, 1), :],
                coords_ref[0, pl.ds(owner, 1), :],
                coords_ref[1, pl.ds(owner, 1), :],
            )
            for comp in range(3):
                part = sums[64 * comp : 64 * comp + 64, LANES * half : LANES * half + LANES]
                places_ref[pl.ds(4 * owner + comp, 1), :] = jnp.sum(
                    part * planar, axis=0, keepdims=True
                )
            places_ref[pl.ds(4 * owner + 3, 1), :] = jnp.zeros((1, LANES), F32)


def fibre_tables_kernel(slots_ref, angles_ref, direction_ref, fibre_ref, node_ref):
    azimuth, elevation = angles_ref[0], angles_ref[1]
    flat = jnp.cos(elevation)
    direction_ref[0] = jnp.cos(azimuth) * flat
    direction_ref[1] = jnp.sin(azimuth) * flat
    direction_ref[2] = jnp.sin(elevation)
    lefts, rights = [], []
    nodes = iota((1, LANES), 1).astype(F32)
    for fibre in range(16):
        slots = slots_ref[pl.ds(fibre, 1), :]
        host = iota((32, LANES), 0) == (slots >> 7)
        lefts.append(
            jnp.concatenate(
                [jnp.where(host, float(fibre + 1), 0.0), jnp.where(host, nodes, 0.0)], axis=0
            ).astype(BF16)
        )
        rights.append((iota((LANES, LANES), 0) == (slots & 127)).astype(F32).astype(BF16))
    table = lax.dot_general(
        jnp.concatenate(lefts, axis=1),
        jnp.concatenate(rights, axis=1),
        (((1,), (1,)), ((), ())),
        preferred_element_type=F32,
    )
    table = table.astype(jnp.int32)
    fibre_ref[...] = table[:32]
    node_ref[...] = table[32:]


def lane_pick(row, index):
    return jnp.take_along_axis(jnp.broadcast_to(row, index.shape), index, axis=1)


def fibre_kernel(
    places_ref, slots_ref, direction_ref, stiffness_ref, fibre_ref, node_ref, pulls_ref
):
    slots = slots_ref[...]
    host, spot = slots >> 7, slots & 127
    places = [jnp.zeros(slots.shape, F32) for _ in range(3)]
    for step in range(32):
        here = host == step
        for comp in range(3):
            picked = lane_pick(places_ref[pl.ds(4 * step + comp, 1), :], spot)
            places[comp] = jnp.where(here, picked, places[comp])
    strain = jnp.zeros(slots.shape, F32)
    for comp in range(3):
        ahead = pltpu.roll(places[comp], LANES - 1, 1)
        strain = strain + direction_ref[comp] * (ahead - places[comp])
    live = iota(slots.shape, 1) < LANES - 1
    tension = jnp.where(live, stiffness_ref[...] * jnp.maximum(strain, 0.0), 0.0)
    forces = []
    for comp in range(3):
        pull = tension * direction_ref[comp]
        forces.append(pull - pltpu.roll(pull, 1, 1))
    for block in range(4):
        fibre = fibre_ref[pl.ds(8 * block, 8), :]
        node = node_ref[pl.ds(8 * block, 8), :]
        placed = [jnp.zeros((8, LANES), F32) for _ in range(3)]
        for step in range(16):
            here = fibre == step + 1
            for comp in range(3):
                picked = lane_pick(forces[comp][step : step + 1], node)
                placed[comp] = jnp.where(here, picked, placed[comp])
        for comp in range(3):
            pulls_ref[pl.ds(32 * block + comp, 8, stride=4), :] = placed[comp]
        pulls_ref[pl.ds(32 * block + 3, 8, stride=4), :] = jnp.zeros((8, LANES), F32)


def side_rows_kernel(
    odd_ref, u_ref, density_ref, modulus_ref, even_in_ref, odd_in_ref, even_ref, odd_swap_ref
):
    odd_dom = odd_ref[0, 0] != 0
    odd_blk = odd_ref[0, 1] != 0
    for comp in range(5):
        lower = jnp.where(odd_dom, even_in_ref[comp], odd_in_ref[comp])
        upper = jnp.where(odd_dom, odd_in_ref[comp], even_in_ref[comp])
        rows = []
        for at in (0, 7):
            if comp < 3:
                own = u_ref[comp, :, at, :]
            else:
                own = (modulus_ref if comp == 3 else density_ref)[:, at, :]
            rows.append(
                jnp.concatenate([lower[at : at + 1], own, upper[at : at + 1]], axis=0)
            )
        first, last = rows
        even_ref[pl.ds(10 * comp, 10), :] = jnp.where(odd_blk, first, last)
        odd_swap_ref[pl.ds(10 * comp, 10), :] = jnp.where(odd_blk, last, first)


def elastic_kernel(
    odd_ref, u_ref, velocity_ref, load_ref, density_ref, modulus_ref,
    even_x_ref, odd_x_ref, even_y_ref, odd_y_ref,
    velocity_out_ref, displacement_out_ref, inverse_mass_ref,
    nodes_ref, depth_ref, corner_ref,
):
    odd_dom = odd_ref[0, 0] != 0
    odd_blk = odd_ref[0, 1] != 0
    for comp in range(5):
        nodes_ref[comp, pl.ds(96, 24), :] = jnp.zeros((24, LANES), F32)
        lower = jnp.where(odd_dom, even_x_ref[comp], odd_x_ref[comp])
        upper = jnp.where(odd_dom, odd_x_ref[comp], even_x_ref[comp])
        nodes_ref[comp, pl.ds(1, 8), :] = lower
        nodes_ref[comp, pl.ds(91, 8), :] = upper
        for x in range(8):
            if comp < 3:
                own = u_ref[comp, x]
            else:
                own = (modulus_ref if comp == 3 else density_ref)[x]
            nodes_ref[comp, pl.ds(10 * x + 11, 8), :] = own
        even = even_y_ref[pl.ds(10 * comp, 10), :]
        odd = odd_y_ref[pl.ds(10 * comp, 10), :]
        left = jnp.where(odd_blk, even, odd)
        right = jnp.where(odd_blk, odd, even)
        for x in range(10):
            nodes_ref[comp, pl.ds(10 * x, 1), :] = left[x : x + 1]
            nodes_ref[comp, pl.ds(10 * x + 9, 1), :] = right[x : x + 1]
    last_lane = iota((8, LANES), 1) == LANES - 1
    first_lane = iota((8, LANES), 1) == 0
    for comp in range(3):
        for chunk in range(ROWS_PAD // 8):
            here = nodes_ref[comp, pl.ds(8 * chunk, 8), :]
            above = jnp.where(last_lane, 0.0, pltpu.roll(here, LANES - 1, 1))
            depth_ref[2 * comp, pl.ds(8 * chunk, 8), :] = above + here
            depth_ref[2 * comp + 1, pl.ds(8 * chunk, 8), :] = above - here

    long, cross, shear = (LAME + 2 * SHEAR) / 16, LAME / 16, SHEAR / 16
    long3, cross3, shear3 = (LAME + 3 * SHEAR) / 48, LAME / 48, SHEAR / 48
    long9 = (LAME + 4 * SHEAR) / 144
    for chunk in range(ROWS // 8):
        at = 8 * chunk
        mode = {}
        for comp in range(3):
            for c in range(2):
                a00 = depth_ref[2 * comp + c, pl.ds(at, 8), :]
                a01 = depth_ref[2 * comp + c, pl.ds(at + 1, 8), :]
                a10 = depth_ref[2 * comp + c, pl.ds(at + 10, 8), :]
                a11 = depth_ref[2 * comp + c, pl.ds(at + 11, 8), :]
                s0, d0, s1, d1 = a00 + a01, a01 - a00, a10 + a11, a11 - a10
                mode[comp, 0, 0, c] = s0 + s1
                mode[comp, 0, 1, c] = d0 + d1
                mode[comp, 1, 0, c] = s1 - s0
                mode[comp, 1, 1, c] = d1 - d0
        scale = nodes_ref[3, pl.ds(at, 8), :]
        u100, v010, w001 = mode[0, 1, 0, 0], mode[1, 0, 1, 0], mode[2, 0, 0, 1]
        trace = cross * (u100 + v010 + w001)
        f = {}
        f[0, 1, 0, 0] = (long - cross) * u100 + trace
        f[1, 0, 1, 0] = (long - cross) * v010 + trace
        f[2, 0, 0, 1] = (long - cross) * w001 + trace
        f[0, 0, 1, 0] = f[1, 1, 0, 0] = shear * (mode[0, 0, 1, 0] + mode[1, 1, 0, 0])
        f[0, 0, 0, 1] = f[2, 1, 0, 0] = shear * (mode[0, 0, 0, 1] + mode[2, 1, 0, 0])
        f[1, 0, 0, 1] = f[2, 0, 1, 0] = shear * (mode[1, 0, 0, 1] + mode[2, 0, 1, 0])
        for one, two in (
            ((0, 1, 1, 0), (2, 0, 1, 1)),
            ((0, 1, 0, 1), (1, 0, 1, 1)),
            ((1, 1, 1, 0), (2, 1, 0, 1)),
        ):
            f[one] = long3 * mode[one] + cross3 * mode[two]
            f[two] = long3 * mode[two] + cross3 * mode[one]
        twist = mode[0, 0, 1, 1] + mode[1, 1, 0, 1] + mode[2, 1, 1, 0]
        for key in ((0, 0, 1, 1), (1, 1, 0, 1), (2, 1, 1, 0)):
            f[key] = shear3 * (twist + mode[key])
        for comp in range(3):
            f[comp, 1, 1, 1] = long9 * mode[comp, 1, 1, 1]
        f = {key: value * scale for key, value in f.items()}
        for comp in range(3):
            for c in range(2):
                m01, m10, m11 = f[comp, 0, 1, c], f[comp, 1, 0, c], f[comp, 1, 1, c]
                total, other = m10 + m01, m10 - m01
                corners = (m11 - total, -m11 - other, other - m11, total + m11)
                if c == 1:
                    m00 = f[comp, 0, 0, 1]
                    corners = tuple(corner + m00 for corner in corners)
                for which in range(4):
                    corner_ref[8 * comp + 4 * c + which, pl.ds(at + 16, 8), :] = corners[which]

    shifts = (0, 1, 10, 11)
    for x in range(8):
        at = 10 * x + 11
        weight = sum(nodes_ref[4, pl.ds(at - shift, 8), :] for shift in shifts)
        below = jnp.where(first_lane, 0.0, pltpu.roll(weight, 1, 1))
        inverse = 1.0 / (0.125 * (weight + below))
        inverse_mass_ref[x] = inverse
        for comp in range(3):
            h0, h1 = (
                sum(
                    corner_ref[8 * comp + 4 * c + which, pl.ds(at + 16 - shift, 8), :]
                    for which, shift in enumerate(shifts)
                )
                for c in range(2)
            )
            below = jnp.where(first_lane, 0.0, pltpu.roll(h0 + h1, 1, 1))
            elastic = h0 - h1 + below
            velocity = velocity_ref[comp, x]
            acceleration = (load_ref[comp, x] - elastic) * inverse - DAMPING * velocity
            velocity = velocity + TIME_STEP * acceleration
            velocity_out_ref[comp, x] = velocity
            displacement_out_ref[comp, x] = u_ref[comp, x] + TIME_STEP * velocity


def spread_kernel(
    pulls_ref, element_ref, coords_ref, high_ref, low_ref,
    velocity_ref, displacement_ref, inverse_mass_ref,
    displacement_out_ref, velocity_out_ref,
):
    total = jnp.zeros((384, 256), F32)
    for pair in range(16):
        highs, lows, weights = [], [], []
        for half in range(2):
            owner = 2 * pair + half
            planar = planar_weights(
                element_ref[pl.ds(owner, 1), :],
                coords_ref[0, pl.ds(owner, 1), :],
                coords_ref[1, pl.ds(owner, 1), :],
            )
            terms = jnp.concatenate(
                [planar * pulls_ref[pl.ds(4 * owner + comp, 1), :] for comp in range(3)], axis=0
            )
            high, low = split(terms)
            highs.append(high)
            lows.append(low)
            weights.append(jnp.concatenate([high_ref[owner], low_ref[owner]], axis=0))
        left = jnp.concatenate(
            [jnp.concatenate(highs, axis=1), jnp.concatenate(lows, axis=1)], axis=0
        )
        total = total + lax.dot_general(
            left,
            jnp.concatenate(weights, axis=1),
            (((1,), (1,)), ((), ())),
            preferred_element_type=F32,
        )
    fibre = (total[:192, :LANES] + total[192:, :LANES]) + (
        total[:192, LANES:] + total[192:, LANES:]
    )
    for comp in range(3):
        for x in range(8):
            row = 64 * comp + 8 * x
            change = TIME_STEP * (fibre[row : row + 8] * inverse_mass_ref[x])
            velocity_out_ref[comp, x] = velocity_ref[comp, x] + change
            displacement_out_ref[comp, x] = displacement_ref[comp, x] + TIME_STEP * change


def call(kernel, outs, scratch=(), scalars=0, inputs=0):
    specs = [pl.BlockSpec(memory_space=pltpu.SMEM)] * scalars
    specs += [pl.BlockSpec(memory_space=pltpu.VMEM)] * inputs
    many = isinstance(outs, (tuple, list))
    vmem = pl.BlockSpec(memory_space=pltpu.VMEM)
    return pl.pallas_call(
        kernel,
        out_shape=outs,
        in_specs=specs,
        out_specs=type(outs)(vmem for _ in outs) if many else vmem,
        scratch_shapes=scratch,
    )


def swap(shard, axis, first):
    size = lax.axis_size(axis)
    pairs = [(i, i + 1) for i in range(first, size - 1, 2)]
    return lax.ppermute(shard, axis, pairs + [(b, a) for a, b in pairs])


def exchange(rows):
    blocks = rows.reshape(32, 4, LANES)
    return lax.all_to_all(blocks, DOM, split_axis=0, concat_axis=0, tiled=True).reshape(
        128, LANES
    )


def shards(
    displacement, velocity, load, density, block_class,
    host_element, host_coords, fibre_slot, fibre_angles, fibre_stiffness,
):
    odd = jnp.stack([lax.axis_index(DOM) % 2, lax.axis_index("blk") % 2]).reshape(1, 2)
    odd = odd.astype(jnp.int32)
    element = host_element.reshape(32, LANES)
    coords = host_coords.reshape(3, 32, LANES)
    slots = fibre_slot.reshape(16, LANES)
    grid = (3, 8, 8, LANES)
    weights = sds((32, LANES, LANES), BF16)
    places, high, low, modulus, even_x, odd_x = call(
        interpolate_kernel,
        (
            sds((128, LANES)), weights, weights, sds((8, 8, LANES)),
            sds((5, 8, LANES)), sds((5, 8, LANES)),
        ),
        scalars=1, inputs=5,
    )(odd, displacement, element, coords, density, block_class.reshape(1, 16))
    received = exchange(places)
    even_x = swap(even_x, DOM, 0)
    odd_x = swap(odd_x, DOM, 1)
    direction, fibre, node = call(
        fibre_tables_kernel,
        (sds((3, 16, LANES)), sds((32, LANES), jnp.int32), sds((32, LANES), jnp.int32)),
        inputs=2,
    )(slots, fibre_angles.reshape(2, 16, LANES))
    even_y, odd_y = call(
        side_rows_kernel, (sds((50, LANES)), sds((50, LANES))), scalars=1, inputs=5
    )(odd, displacement, density, modulus, even_x, odd_x)
    even_y = swap(even_y, "blk", 0)
    odd_y = swap(odd_y, "blk", 1)
    pulls = call(fibre_kernel, sds((128, LANES)), inputs=6)(
        received, slots, direction, fibre_stiffness.reshape(16, 1), fibre, node
    )
    returned = exchange(pulls)
    step_velocity, step_displacement, inverse_mass = call(
        elastic_kernel,
        (sds(grid), sds(grid), sds((8, 8, LANES))),
        scratch=(
            pltpu.VMEM((5, ROWS_PAD, LANES), F32),
            pltpu.VMEM((6, ROWS_PAD, LANES), F32),
            pltpu.VMEM((24, ROWS_PAD, LANES), F32),
        ),
        scalars=1, inputs=9,
    )(odd, displacement, velocity, load, density, modulus, even_x, odd_x, even_y, odd_y)
    return call(spread_kernel, (sds(grid), sds(grid)), inputs=8)(
        returned, element, coords, high, low, step_velocity, step_displacement, inverse_mass
    )


def solution(mesh):
    finer = Mesh(
        mesh.devices.reshape(4, 4, 2, mesh.shape["blk"]), ("dom_0", "dom_1", "dom_2", "blk")
    )
    in_specs = (
        P(None, DOM, "blk", None),
        P(None, DOM, "blk", None),
        P(None, DOM, "blk", None),
        P(DOM, "blk", None),
        P(DOM, "blk", None),
        P("blk", DOM),
        P(None, "blk", DOM),
        P(DOM, "blk", None),
        P(None, DOM, "blk", None),
        P(DOM, "blk"),
    )
    out_specs = (P(None, DOM, "blk", None), P(None, DOM, "blk", None))
    return jax.shard_map(
        shards, mesh=finer, in_specs=in_specs, out_specs=out_specs, check_vma=False
    )
```

```python
import jax
import jax.numpy as jnp
from jax import lax
from jax.experimental import pallas as pl
from jax.experimental.pallas import tpu as pltpu
from jax.sharding import Mesh
from jax.sharding import PartitionSpec as P

DOM = ("dom_0", "dom_1", "dom_2")
CLASS_VALUES = (1.0, 0.45, 0.12)
TIME_STEP = 0.25
DAMPING = 0.5
LAME = 0.3 / (1.3 * 0.4)
SHEAR = 0.5 / 1.3

F32 = jnp.float32
BF16 = jnp.bfloat16
LANES = 128
ROWS = 104
ROWS_PAD = 120


def odd_dom_index():
    return lax.axis_index("dom_2") == 1


def odd_blk_index():
    return (lax.axis_index("blk") & 1) == 1


def split(value):
    high = value.astype(BF16)
    low = (value - high.astype(F32)).astype(BF16)
    return high, low


def iota(shape, axis):
    return lax.broadcasted_iota(jnp.int32, shape, axis)


def hat(lowest, along, count):
    where = iota((count, LANES), 0)
    return jnp.where(
        where == lowest, 1.0 - along, jnp.where(where == lowest + 1, along, 0.0)
    )


def planar_weights(element, along_r, along_p):
    weight_x = hat(element >> 10, along_r, 8)
    weight_y = hat((element >> 7) & 7, along_p, 8)
    return (weight_x[:, None, :] * weight_y[None]).reshape(64, LANES)


def interpolate_kernel(*refs):
    count = (len(refs) - 5) // 2
    sources, places_ref, modulus_ref, even_ref, odd_swap_ref = refs[:count], *refs[count : count + 4]
    targets, semaphores = refs[count + 4 : -1], refs[-1]
    copies = [
        pltpu.make_async_copy(source, target, semaphores.at[index])
        for index, (source, target) in enumerate(zip(sources, targets))
    ]
    for copy in copies:
        copy.start()
    u_ref, element_ref, coords_ref, density_ref, class_ref = targets[:5]
    for copy in copies[:5]:
        copy.wait()
    lane_block = iota((16, LANES), 1) >> 3
    pick = (lane_block == iota((16, LANES), 0)).astype(F32)
    kind = jnp.dot(
        jnp.broadcast_to(class_ref[...].astype(F32), (8, 16)), pick, preferred_element_type=F32
    )
    factor = jnp.zeros((8, LANES), F32)
    for index, value in enumerate(CLASS_VALUES):
        factor = factor + jnp.where(kind == float(index), value, 0.0)
    density = density_ref[...]
    modulus = factor[None] * density * density
    modulus_ref[...] = modulus
    odd = odd_dom_index()
    for comp in range(5):
        if comp < 3:
            first, last = u_ref[comp, 0], u_ref[comp, 7]
        else:
            source = modulus if comp == 3 else density
            first, last = source[0], source[7]
        even_ref[comp] = jnp.where(odd, first, last)
        odd_swap_ref[comp] = jnp.where(odd, last, first)

    field_high, field_low = split(u_ref[...].reshape(192, LANES))
    field = jnp.concatenate([field_high, field_low], axis=1)
    for pair in range(16):
        highs, lows = [], []
        for half in range(2):
            owner = 2 * pair + half
            element = element_ref[pl.ds(owner, 1), :]
            weight_z = hat(element & 127, coords_ref[2, pl.ds(owner, 1), :], LANES)
            high, low = split(weight_z)
            highs.append(high)
            lows.append(low)
        high = jnp.concatenate(highs, axis=1)
        low = jnp.concatenate(lows, axis=1)
        sums = jnp.dot(
            field, jnp.concatenate([high, high], axis=0), preferred_element_type=F32
        ) + jnp.dot(field_high, low, preferred_element_type=F32)
        for half in range(2):
            owner = 2 * pair + half
            planar = planar_weights(
                element_ref[pl.ds(owner, 1), :],
                coords_ref[0, pl.ds(owner, 1), :],
                coords_ref[1, pl.ds(owner, 1), :],
            )
            for comp in range(3):
                part = sums[64 * comp : 64 * comp + 64, LANES * half : LANES * half + LANES]
                places_ref[pl.ds(4 * owner + comp, 1), :] = jnp.sum(
                    part * planar, axis=0, keepdims=True
                )
            places_ref[pl.ds(4 * owner + 3, 1), :] = jnp.zeros((1, LANES), F32)
    for copy in copies[5:]:
        copy.wait()


def weights_kernel(element_ref, coords_ref, depth_ref, weight_x_ref, weight_y_ref):
    lowest, along = element_ref[...] >> 10, coords_ref[0]
    for x in range(8):
        weight_x_ref[x] = jnp.where(
            lowest == x, 1.0 - along, jnp.where(lowest == x - 1, along, 0.0)
        )
    for owner in range(32):
        element = element_ref[pl.ds(owner, 1), :]
        high, low = split(hat(element & 127, coords_ref[2, pl.ds(owner, 1), :], LANES))
        depth_ref[pl.ds(0, LANES), pl.ds(LANES * owner, LANES)] = high
        depth_ref[pl.ds(LANES, LANES), pl.ds(LANES * owner, LANES)] = low
        weight_y_ref[owner] = hat((element >> 7) & 7, coords_ref[1, pl.ds(owner, 1), :], 8)


def fibre_tables_kernel(
    slots_ref, angles_ref, stiffness_ref, direction_ref, stiff_ref, fibre_ref, node_ref
):
    square = iota((16, 16), 0) == iota((16, 16), 1)
    stiffness = jnp.sum(jnp.where(square, stiffness_ref[...], 0.0), axis=1, keepdims=True)
    stiff_ref[...] = jnp.where(iota((16, LANES), 1) < LANES - 1, stiffness, 0.0)
    azimuth, elevation = angles_ref[0], angles_ref[1]
    flat = jnp.cos(elevation)
    direction_ref[0] = jnp.cos(azimuth) * flat
    direction_ref[1] = jnp.sin(azimuth) * flat
    direction_ref[2] = jnp.sin(elevation)
    lefts, rights = [], []
    nodes = iota((1, LANES), 1).astype(F32)
    for fibre in range(16):
        slots = slots_ref[pl.ds(fibre, 1), :]
        host = iota((32, LANES), 0) == (slots >> 7)
        lefts.append(
            jnp.concatenate(
                [jnp.where(host, float(fibre + 1), 0.0), jnp.where(host, nodes, 0.0)], axis=0
            ).astype(BF16)
        )
        rights.append((iota((LANES, LANES), 0) == (slots & 127)).astype(F32).astype(BF16))
    table = lax.dot_general(
        jnp.concatenate(lefts, axis=1),
        jnp.concatenate(rights, axis=1),
        (((1,), (1,)), ((), ())),
        preferred_element_type=F32,
    )
    table = table.astype(jnp.int32)
    fibre_ref[...] = table[:32]
    node_ref[...] = table[32:]


def lane_pick(row, index):
    return jnp.take_along_axis(jnp.broadcast_to(row, index.shape), index, axis=1)


def fibre_kernel(
    places_ref, slots_ref, direction_ref, stiff_ref, fibre_ref, node_ref, pulls_ref
):
    slots = slots_ref[...]
    host, spot = slots >> 7, slots & 127
    places = [jnp.zeros(slots.shape, F32) for _ in range(3)]
    for step in range(32):
        here = host == step
        for comp in range(3):
            picked = lane_pick(places_ref[pl.ds(4 * step + comp, 1), :], spot)
            places[comp] = jnp.where(here, picked, places[comp])
    strain = jnp.zeros(slots.shape, F32)
    for comp in range(3):
        ahead = pltpu.roll(places[comp], LANES - 1, 1)
        strain = strain + direction_ref[comp] * (ahead - places[comp])
    tension = stiff_ref[...] * jnp.maximum(strain, 0.0)
    forces = []
    for comp in range(3):
        pull = tension * direction_ref[comp]
        forces.append(pull - pltpu.roll(pull, 1, 1))
    for block in range(4):
        fibre = fibre_ref[pl.ds(8 * block, 8), :]
        node = node_ref[pl.ds(8 * block, 8), :]
        placed = [jnp.zeros((8, LANES), F32) for _ in range(3)]
        for step in range(16):
            here = fibre == step + 1
            for comp in range(3):
                picked = lane_pick(forces[comp][step : step + 1], node)
                placed[comp] = jnp.where(here, picked, placed[comp])
        for comp in range(3):
            pulls_ref[pl.ds(32 * block + comp, 8, stride=4), :] = placed[comp]
        pulls_ref[pl.ds(32 * block + 3, 8, stride=4), :] = jnp.zeros((8, LANES), F32)


def side_rows_kernel(
    u_ref, density_ref, modulus_ref, even_in_ref, odd_in_ref, even_ref, odd_swap_ref
):
    odd_dom = odd_dom_index()
    odd_blk = odd_blk_index()
    for comp in range(5):
        lower = jnp.where(odd_dom, even_in_ref[comp], odd_in_ref[comp])
        upper = jnp.where(odd_dom, odd_in_ref[comp], even_in_ref[comp])
        rows = []
        for at in (0, 7):
            if comp < 3:
                own = u_ref[comp, :, at, :]
            else:
                own = (modulus_ref if comp == 3 else density_ref)[:, at, :]
            rows.append(
                jnp.concatenate([lower[at : at + 1], own, upper[at : at + 1]], axis=0)
            )
        first, last = rows
        even_ref[pl.ds(10 * comp, 10), :] = jnp.where(odd_blk, first, last)
        odd_swap_ref[pl.ds(10 * comp, 10), :] = jnp.where(odd_blk, last, first)


def elastic_kernel(
    u_ref, velocity_ref, load_ref, density_ref, modulus_ref,
    even_x_ref, odd_x_ref, even_y_ref, odd_y_ref,
    velocity_out_ref, displacement_out_ref, inverse_mass_ref,
    nodes_ref, depth_ref, corner_ref,
):
    odd_dom = odd_dom_index()
    odd_blk = odd_blk_index()
    for comp in range(5):
        nodes_ref[comp, pl.ds(96, 24), :] = jnp.zeros((24, LANES), F32)
        lower = jnp.where(odd_dom, even_x_ref[comp], odd_x_ref[comp])
        upper = jnp.where(odd_dom, odd_x_ref[comp], even_x_ref[comp])
        nodes_ref[comp, pl.ds(1, 8), :] = lower
        nodes_ref[comp, pl.ds(91, 8), :] = upper
        for x in range(8):
            if comp < 3:
                own = u_ref[comp, x]
            else:
                own = (modulus_ref if comp == 3 else density_ref)[x]
            nodes_ref[comp, pl.ds(10 * x + 11, 8), :] = own
        even = even_y_ref[pl.ds(10 * comp, 10), :]
        odd = odd_y_ref[pl.ds(10 * comp, 10), :]
        left = jnp.where(odd_blk, even, odd)
        right = jnp.where(odd_blk, odd, even)
        for x in range(10):
            nodes_ref[comp, pl.ds(10 * x, 1), :] = left[x : x + 1]
            nodes_ref[comp, pl.ds(10 * x + 9, 1), :] = right[x : x + 1]
    last_lane = iota((8, LANES), 1) == LANES - 1
    first_lane = iota((8, LANES), 1) == 0
    for comp in range(3):
        for chunk in range(ROWS_PAD // 8):
            here = nodes_ref[comp, pl.ds(8 * chunk, 8), :]
            above = jnp.where(last_lane, 0.0, pltpu.roll(here, LANES - 1, 1))
            depth_ref[2 * comp, pl.ds(8 * chunk, 8), :] = above + here
            depth_ref[2 * comp + 1, pl.ds(8 * chunk, 8), :] = above - here

    long, cross, shear = (LAME + 2 * SHEAR) / 16, LAME / 16, SHEAR / 16
    long3, cross3, shear3 = (LAME + 3 * SHEAR) / 48, LAME / 48, SHEAR / 48
    long9 = (LAME + 4 * SHEAR) / 144
    for chunk in range(ROWS // 8):
        at = 8 * chunk
        mode = {}
        for comp in range(3):
            for c in range(2):
                a00 = depth_ref[2 * comp + c, pl.ds(at, 8), :]
                a01 = depth_ref[2 * comp + c, pl.ds(at + 1, 8), :]
                a10 = depth_ref[2 * comp + c, pl.ds(at + 10, 8), :]
                a11 = depth_ref[2 * comp + c, pl.ds(at + 11, 8), :]
                s0, d0, s1, d1 = a00 + a01, a01 - a00, a10 + a11, a11 - a10
                mode[comp, 0, 0, c] = s0 + s1
                mode[comp, 0, 1, c] = d0 + d1
                mode[comp, 1, 0, c] = s1 - s0
                mode[comp, 1, 1, c] = d1 - d0
        scale = nodes_ref[3, pl.ds(at, 8), :]
        u100, v010, w001 = mode[0, 1, 0, 0], mode[1, 0, 1, 0], mode[2, 0, 0, 1]
        trace = cross * (u100 + v010 + w001)
        f = {}
        f[0, 1, 0, 0] = (long - cross) * u100 + trace
        f[1, 0, 1, 0] = (long - cross) * v010 + trace
        f[2, 0, 0, 1] = (long - cross) * w001 + trace
        f[0, 0, 1, 0] = f[1, 1, 0, 0] = shear * (mode[0, 0, 1, 0] + mode[1, 1, 0, 0])
        f[0, 0, 0, 1] = f[2, 1, 0, 0] = shear * (mode[0, 0, 0, 1] + mode[2, 1, 0, 0])
        f[1, 0, 0, 1] = f[2, 0, 1, 0] = shear * (mode[1, 0, 0, 1] + mode[2, 0, 1, 0])
        for one, two in (
            ((0, 1, 1, 0), (2, 0, 1, 1)),
            ((0, 1, 0, 1), (1, 0, 1, 1)),
            ((1, 1, 1, 0), (2, 1, 0, 1)),
        ):
            f[one] = long3 * mode[one] + cross3 * mode[two]
            f[two] = long3 * mode[two] + cross3 * mode[one]
        twist = mode[0, 0, 1, 1] + mode[1, 1, 0, 1] + mode[2, 1, 1, 0]
        for key in ((0, 0, 1, 1), (1, 1, 0, 1), (2, 1, 1, 0)):
            f[key] = shear3 * (twist + mode[key])
        for comp in range(3):
            f[comp, 1, 1, 1] = long9 * mode[comp, 1, 1, 1]
        f = {key: value * scale for key, value in f.items()}
        for comp in range(3):
            for c in range(2):
                m01, m10, m11 = f[comp, 0, 1, c], f[comp, 1, 0, c], f[comp, 1, 1, c]
                total, other = m10 + m01, m10 - m01
                corners = (m11 - total, -m11 - other, other - m11, total + m11)
                if c == 1:
                    m00 = f[comp, 0, 0, 1]
                    corners = tuple(corner + m00 for corner in corners)
                for which in range(4):
                    corner_ref[8 * comp + 4 * c + which, pl.ds(at + 16, 8), :] = corners[which]

    shifts = (0, 1, 10, 11)
    for x in range(8):
        at = 10 * x + 11
        weight = sum(nodes_ref[4, pl.ds(at - shift, 8), :] for shift in shifts)
        below = jnp.where(first_lane, 0.0, pltpu.roll(weight, 1, 1))
        inverse = 1.0 / (0.125 * (weight + below))
        inverse_mass_ref[x] = inverse
        for comp in range(3):
            h0, h1 = (
                sum(
                    corner_ref[8 * comp + 4 * c + which, pl.ds(at + 16 - shift, 8), :]
                    for which, shift in enumerate(shifts)
                )
                for c in range(2)
            )
            below = jnp.where(first_lane, 0.0, pltpu.roll(h0 + h1, 1, 1))
            elastic = h0 - h1 + below
            velocity = velocity_ref[comp, x]
            acceleration = (load_ref[comp, x] - elastic) * inverse - DAMPING * velocity
            velocity = velocity + TIME_STEP * acceleration
            velocity_out_ref[comp, x] = velocity
            displacement_out_ref[comp, x] = u_ref[comp, x] + TIME_STEP * velocity


def spread_kernel(
    pulls_ref, depth_ref, weight_x_ref, weight_y_ref,
    velocity_ref, displacement_ref, inverse_mass_ref,
    displacement_out_ref, velocity_out_ref, terms_ref,
):
    for owner in range(32):
        at = pl.ds(LANES * owner, LANES)
        weight_y = weight_y_ref[owner]
        planar = jnp.concatenate(
            [weight_y * weight_x_ref[x, pl.ds(owner, 1), :] for x in range(8)], axis=0
        )
        for comp in range(3):
            high, low = split(planar * pulls_ref[pl.ds(4 * owner + comp, 1), :])
            terms_ref[pl.ds(64 * comp, 64), at] = high
            terms_ref[pl.ds(192 + 64 * comp, 64), at] = low
    total = lax.dot_general(
        terms_ref[...], depth_ref[...], (((1,), (1,)), ((), ())), preferred_element_type=F32
    )
    fibre = (total[:192, :LANES] + total[192:, :LANES]) + (
        total[:192, LANES:] + total[192:, LANES:]
    )
    for comp in range(3):
        for x in range(8):
            row = 64 * comp + 8 * x
            change = TIME_STEP * (fibre[row : row + 8] * inverse_mass_ref[x])
            velocity_out_ref[comp, x] = velocity_ref[comp, x] + change
            displacement_out_ref[comp, x] = displacement_ref[comp, x] + TIME_STEP * change


VMEM = pl.BlockSpec(memory_space=pltpu.VMEM)


def call(kernel, outs, ins, scratch=(), final=False, first=False):
    space = jax.ShapeDtypeStruct if final else pltpu.VMEM
    outs = tuple(space(shape, dtype) for shape, dtype in outs)
    space_in = pltpu.HBM if first else pltpu.VMEM
    ins = tuple(pltpu.with_memory_space_constraint(value, space_in) for value in ins)
    return pl.pallas_call(
        kernel,
        out_shape=outs,
        in_specs=[pl.BlockSpec(memory_space=space_in)] * len(ins),
        out_specs=(VMEM,) * len(outs),
        scratch_shapes=scratch,
        compiler_params=pltpu.CompilerParams(vmem_limit_bytes=16 << 20),
    )(*ins)


def swap(shard, axis, first):
    size = lax.axis_size(axis)
    pairs = [(i, i + 1) for i in range(first, size - 1, 2)]
    return lax.ppermute(shard, axis, pairs + [(b, a) for a, b in pairs])


def exchange(rows):
    blocks = rows.reshape(32, 4, LANES)
    blocks = lax.all_to_all(blocks, DOM, split_axis=0, concat_axis=0, tiled=True)
    return blocks.reshape(128, LANES)


def step(
    displacement, velocity, load, density, block_class,
    host_element, host_coords, fibre_slot, fibre_angles, fibre_stiffness,
):
    grid = (3, 8, 8, LANES)
    plane = (8, 8, LANES)
    side = ((50, LANES), F32)
    arguments = (
        displacement,
        host_element.reshape(32, LANES),
        host_coords.reshape(3, 32, LANES),
        density,
        block_class.reshape(1, 16),
        velocity,
        load,
        fibre_slot.reshape(16, LANES),
        fibre_angles.reshape(2, 16, LANES),
        fibre_stiffness.reshape(1, 16),
    )
    places, modulus, even_x, odd_x, *arguments = call(
        interpolate_kernel,
        (((128, LANES), F32), (plane, F32), ((5, 8, LANES), F32), ((5, 8, LANES), F32))
        + tuple((value.shape, value.dtype) for value in arguments),
        arguments,
        scratch=(pltpu.SemaphoreType.DMA((len(arguments),)),),
        first=True,
    )
    displacement, element, coords, density, _, velocity, load, slots, angles, stiffness = arguments
    even_x = swap(even_x, DOM, 0)
    odd_x = swap(odd_x, DOM, 1)
    received = exchange(places)
    table = ((32, LANES), jnp.int32)
    direction, stiff, fibre, node = call(
        fibre_tables_kernel,
        (((3, 16, LANES), F32), ((16, LANES), F32), table, table),
        (slots, angles, stiffness),
    )
    even_y, odd_y = call(
        side_rows_kernel, (side, side), (displacement, density, modulus, even_x, odd_x)
    )
    even_y = swap(even_y, "blk", 0)
    odd_y = swap(odd_y, "blk", 1)
    (pulls,) = call(
        fibre_kernel, (((128, LANES), F32),),
        (received, slots, direction, stiff, fibre, node),
    )
    returned = exchange(pulls)
    depth, weight_x, weight_y = call(
        weights_kernel,
        (((256, 4096), BF16), ((8, 32, LANES), F32), ((32, 8, LANES), F32)),
        (element, coords),
    )
    new_velocity, new_displacement, inverse_mass = call(
        elastic_kernel,
        ((grid, F32), (grid, F32), (plane, F32)),
        (
            displacement, velocity, load, density, modulus,
            even_x, odd_x, even_y, odd_y,
        ),
        scratch=(
            pltpu.VMEM((5, ROWS_PAD, LANES), F32),
            pltpu.VMEM((6, ROWS_PAD, LANES), F32),
            pltpu.VMEM((24, ROWS_PAD, LANES), F32),
        ),
    )
    return call(
        spread_kernel, ((grid, F32), (grid, F32)),
        (returned, depth, weight_x, weight_y, new_velocity, new_displacement, inverse_mass),
        scratch=(pltpu.VMEM((384, 4096), BF16),),
        final=True,
    )


def solution(mesh):
    finer = Mesh(
        mesh.devices.reshape(4, 4, 2, mesh.shape["blk"]), ("dom_0", "dom_1", "dom_2", "blk")
    )
    in_specs = (
        P(None, DOM, "blk", None),
        P(None, DOM, "blk", None),
        P(None, DOM, "blk", None),
        P(DOM, "blk", None),
        P(DOM, "blk", None),
        P("blk", DOM),
        P(None, "blk", DOM),
        P(DOM, "blk", None),
        P(None, DOM, "blk", None),
        P(DOM, "blk"),
    )
    out_specs = (P(None, DOM, "blk", None), P(None, DOM, "blk", None))
    return jax.shard_map(step, mesh=finer, in_specs=in_specs, out_specs=out_specs, check_vma=False)
```

```python
import jax
import jax.numpy as jnp
from jax import lax
from jax.experimental import pallas as pl
from jax.experimental.pallas import tpu as pltpu
from jax.sharding import Mesh
from jax.sharding import PartitionSpec as P

DOM = ("dom_0", "dom_1", "dom_2")
CLASS_VALUES = (1.0, 0.45, 0.12)
TIME_STEP = 0.25
DAMPING = 0.5
LAME = 0.3 / (1.3 * 0.4)
SHEAR = 0.5 / 1.3

F32 = jnp.float32
BF16 = jnp.bfloat16
LANES = 128
ROWS = 104
ROWS_PAD = 120


def odd_dom_index():
    return lax.axis_index("dom_2") == 1


def odd_blk_index():
    return (lax.axis_index("blk") & 1) == 1


def split(value):
    high = value.astype(BF16)
    low = (value - high.astype(F32)).astype(BF16)
    return high, low


def iota(shape, axis):
    return lax.broadcasted_iota(jnp.int32, shape, axis)


def hat(lowest, along, count):
    where = iota((count, LANES), 0)
    return jnp.where(
        where == lowest, 1.0 - along, jnp.where(where == lowest + 1, along, 0.0)
    )


def depth_weights(element, along):
    shape = (LANES, LANES)
    lowest = jnp.broadcast_to(element & (LANES - 1), shape).astype(jnp.int16)
    where = lax.broadcasted_iota(jnp.int16, shape, 0)
    here, above = where == lowest, where == lowest + jnp.int16(1)
    zero = jnp.zeros(shape, BF16)
    parts = []
    for lower, upper in zip(split(1.0 - along), split(along)):
        lower = jnp.broadcast_to(lower.astype(F32), shape).astype(BF16)
        upper = jnp.broadcast_to(upper.astype(F32), shape).astype(BF16)
        parts.append(jnp.where(here, lower, jnp.where(above, upper, zero)))
    return parts


def interpolate_kernel(*refs):
    count = (len(refs) - 7) // 2
    sources, targets, semaphores = refs[:count], refs[count + 6 : -1], refs[-1]
    places_ref, modulus_ref, even_ref, odd_ref, weight_x_ref, weight_y_ref = refs[
        count : count + 6
    ]
    copies = [
        pltpu.make_async_copy(source, target, semaphores.at[index])
        for index, (source, target) in enumerate(zip(sources, targets))
    ]
    for copy in copies:
        copy.start()
    u_ref, element_ref, coords_ref, density_ref, class_ref = targets[:5]
    for copy in copies[:5]:
        copy.wait()
    lowest, along = element_ref[...] >> 10, coords_ref[0]
    for x in range(8):
        weight_x_ref[x] = jnp.where(
            lowest == x, 1.0 - along, jnp.where(lowest == x - 1, along, 0.0)
        )
    field_high, field_low = split(u_ref[...].reshape(192, LANES))
    field = jnp.concatenate([field_high, field_low, field_high], axis=1)
    for pair in range(16):
        parts = []
        for owner in (2 * pair, 2 * pair + 1):
            row = pl.ds(owner, 1)
            high, low = depth_weights(element_ref[row, :], coords_ref[2, row, :])
            parts.append(jnp.concatenate([high, high, low], axis=0))
        sums = jnp.dot(field, jnp.concatenate(parts, axis=1), preferred_element_type=F32)
        for half in range(2):
            owner = 2 * pair + half
            row = pl.ds(owner, 1)
            weight_y = hat((element_ref[row, :] >> 7) & 7, coords_ref[1, row, :], 8)
            weight_y_ref[owner] = weight_y
            rows = [weight_x_ref[x, row, :] for x in range(8)]
            for comp in range(3):
                total = sum(
                    sums[64 * comp + 8 * x :, LANES * half : LANES * half + LANES][:8] * rows[x]
                    for x in range(8)
                )
                places_ref[pl.ds(4 * owner + comp, 1), :] = jnp.sum(
                    total * weight_y, axis=0, keepdims=True
                )
            places_ref[pl.ds(4 * owner + 3, 1), :] = jnp.zeros((1, LANES), F32)

    lane_block = iota((16, LANES), 1) >> 3
    pick = (lane_block == iota((16, LANES), 0)).astype(F32)
    kind = jnp.dot(
        jnp.broadcast_to(class_ref[...].astype(F32), (8, 16)), pick, preferred_element_type=F32
    )
    factor = jnp.zeros((8, LANES), F32)
    for index, value in enumerate(CLASS_VALUES):
        factor = factor + jnp.where(kind == float(index), value, 0.0)
    density = density_ref[...]
    modulus_ref[...] = factor[None] * density * density
    odd_blk = odd_blk_index()
    for comp in range(5):
        source = modulus_ref if comp == 3 else density_ref if comp == 4 else u_ref.at[comp]
        first, last = source[:, 0, :], source[:, 7, :]
        even_ref[comp] = jnp.where(odd_blk, first, last)
        odd_ref[comp] = jnp.where(odd_blk, last, first)
    for copy in copies[5:]:
        copy.wait()


def weights_kernel(element_ref, coords_ref, depth_ref):
    for owner in range(32):
        row = pl.ds(owner, 1)
        high, low = depth_weights(element_ref[row, :], coords_ref[2, row, :])
        depth_ref[owner, pl.ds(0, LANES), :] = high
        depth_ref[owner, pl.ds(LANES, LANES), :] = low


def fibre_tables_kernel(
    slots_ref, angles_ref, stiffness_ref, direction_ref, stiff_ref, fibre_ref, node_ref
):
    square = iota((16, 16), 0) == iota((16, 16), 1)
    stiffness = jnp.sum(jnp.where(square, stiffness_ref[...], 0.0), axis=1, keepdims=True)
    stiff_ref[...] = jnp.where(iota((16, LANES), 1) < LANES - 1, stiffness, 0.0)
    azimuth, elevation = angles_ref[0], angles_ref[1]
    flat = jnp.cos(elevation)
    direction_ref[0] = jnp.cos(azimuth) * flat
    direction_ref[1] = jnp.sin(azimuth) * flat
    direction_ref[2] = jnp.sin(elevation)
    lefts, rights = [], []
    nodes = iota((1, LANES), 1).astype(F32)
    for fibre in range(16):
        slots = slots_ref[pl.ds(fibre, 1), :]
        host = iota((32, LANES), 0) == (slots >> 7)
        lefts.append(
            jnp.concatenate(
                [jnp.where(host, float(fibre + 1), 0.0), jnp.where(host, nodes, 0.0)], axis=0
            ).astype(BF16)
        )
        rights.append((iota((LANES, LANES), 0) == (slots & 127)).astype(F32).astype(BF16))
    table = lax.dot_general(
        jnp.concatenate(lefts, axis=1),
        jnp.concatenate(rights, axis=1),
        (((1,), (1,)), ((), ())),
        preferred_element_type=F32,
    )
    table = table.astype(jnp.int32)
    fibre_ref[...] = table[:32]
    node_ref[...] = table[32:]


def lane_pick(row, index):
    return jnp.take_along_axis(jnp.broadcast_to(row, index.shape), index, axis=1)


def fibre_kernel(
    places_ref, slots_ref, direction_ref, stiff_ref, fibre_ref, node_ref, pulls_ref
):
    slots = slots_ref[...]
    host, spot = slots >> 7, slots & 127
    places = [jnp.zeros(slots.shape, F32) for _ in range(3)]
    for step in range(32):
        here = host == step
        for comp in range(3):
            picked = lane_pick(places_ref[pl.ds(4 * step + comp, 1), :], spot)
            places[comp] = jnp.where(here, picked, places[comp])
    strain = jnp.zeros(slots.shape, F32)
    for comp in range(3):
        ahead = pltpu.roll(places[comp], LANES - 1, 1)
        strain = strain + direction_ref[comp] * (ahead - places[comp])
    tension = stiff_ref[...] * jnp.maximum(strain, 0.0)
    forces = []
    for comp in range(3):
        pull = tension * direction_ref[comp]
        forces.append(pull - pltpu.roll(pull, 1, 1))
    for block in range(4):
        fibre = fibre_ref[pl.ds(8 * block, 8), :]
        node = node_ref[pl.ds(8 * block, 8), :]
        placed = [jnp.zeros((8, LANES), F32) for _ in range(3)]
        for step in range(16):
            here = fibre == step + 1
            for comp in range(3):
                picked = lane_pick(forces[comp][step : step + 1], node)
                placed[comp] = jnp.where(here, picked, placed[comp])
        for comp in range(3):
            pulls_ref[pl.ds(32 * block + comp, 8, stride=4), :] = placed[comp]
        pulls_ref[pl.ds(32 * block + 3, 8, stride=4), :] = jnp.zeros((8, LANES), F32)


def sides_kernel(u_ref, density_ref, modulus_ref, even_y_ref, odd_y_ref, even_ref, odd_ref):
    odd_dom, odd_blk = odd_dom_index(), odd_blk_index()
    for comp in range(5):
        left = jnp.where(odd_blk, even_y_ref[comp], odd_y_ref[comp])
        right = jnp.where(odd_blk, odd_y_ref[comp], even_y_ref[comp])
        source = modulus_ref if comp == 3 else density_ref if comp == 4 else u_ref.at[comp]
        first, last = (
            jnp.concatenate([left[at : at + 1], source[at], right[at : at + 1]], axis=0)
            for at in (0, 7)
        )
        even_ref[pl.ds(10 * comp, 10), :] = jnp.where(odd_dom, first, last)
        odd_ref[pl.ds(10 * comp, 10), :] = jnp.where(odd_dom, last, first)


def elastic_kernel(
    u_ref, velocity_ref, load_ref, density_ref, modulus_ref,
    even_x_ref, odd_x_ref, even_y_ref, odd_y_ref,
    velocity_out_ref, displacement_out_ref, inverse_mass_ref,
    nodes_ref, depth_ref, corner_ref,
):
    odd_dom = odd_dom_index()
    odd_blk = odd_blk_index()
    for comp in range(5):
        nodes_ref[comp, pl.ds(96, 24), :] = jnp.zeros((24, LANES), F32)
        even, odd = even_x_ref[pl.ds(10 * comp, 10), :], odd_x_ref[pl.ds(10 * comp, 10), :]
        nodes_ref[comp, pl.ds(0, 10), :] = jnp.where(odd_dom, even, odd)
        nodes_ref[comp, pl.ds(90, 10), :] = jnp.where(odd_dom, odd, even)
        left = jnp.where(odd_blk, even_y_ref[comp], odd_y_ref[comp])
        right = jnp.where(odd_blk, odd_y_ref[comp], even_y_ref[comp])
        source = modulus_ref if comp == 3 else density_ref if comp == 4 else u_ref.at[comp]
        for x in range(8):
            nodes_ref[comp, pl.ds(10 * x + 10, 1), :] = left[x : x + 1]
            nodes_ref[comp, pl.ds(10 * x + 11, 8), :] = source[x]
            nodes_ref[comp, pl.ds(10 * x + 19, 1), :] = right[x : x + 1]
    last_lane = iota((8, LANES), 1) == LANES - 1
    first_lane = iota((8, LANES), 1) == 0
    for comp in range(3):
        for chunk in range(ROWS_PAD // 8):
            here = nodes_ref[comp, pl.ds(8 * chunk, 8), :]
            above = jnp.where(last_lane, 0.0, pltpu.roll(here, LANES - 1, 1))
            depth_ref[2 * comp, pl.ds(8 * chunk, 8), :] = above + here
            depth_ref[2 * comp + 1, pl.ds(8 * chunk, 8), :] = above - here

    long, cross, shear = (LAME + 2 * SHEAR) / 16, LAME / 16, SHEAR / 16
    long3, cross3, shear3 = (LAME + 3 * SHEAR) / 48, LAME / 48, SHEAR / 48
    long9 = (LAME + 4 * SHEAR) / 144
    for chunk in range(ROWS // 8):
        at = 8 * chunk
        mode = {}
        for comp in range(3):
            for c in range(2):
                a00 = depth_ref[2 * comp + c, pl.ds(at, 8), :]
                a01 = depth_ref[2 * comp + c, pl.ds(at + 1, 8), :]
                a10 = depth_ref[2 * comp + c, pl.ds(at + 10, 8), :]
                a11 = depth_ref[2 * comp + c, pl.ds(at + 11, 8), :]
                s0, d0, s1, d1 = a00 + a01, a01 - a00, a10 + a11, a11 - a10
                mode[comp, 0, 0, c] = s0 + s1
                mode[comp, 0, 1, c] = d0 + d1
                mode[comp, 1, 0, c] = s1 - s0
                mode[comp, 1, 1, c] = d1 - d0
        scale = nodes_ref[3, pl.ds(at, 8), :]
        u100, v010, w001 = mode[0, 1, 0, 0], mode[1, 0, 1, 0], mode[2, 0, 0, 1]
        trace = cross * (u100 + v010 + w001)
        f = {}
        f[0, 1, 0, 0] = (long - cross) * u100 + trace
        f[1, 0, 1, 0] = (long - cross) * v010 + trace
        f[2, 0, 0, 1] = (long - cross) * w001 + trace
        f[0, 0, 1, 0] = f[1, 1, 0, 0] = shear * (mode[0, 0, 1, 0] + mode[1, 1, 0, 0])
        f[0, 0, 0, 1] = f[2, 1, 0, 0] = shear * (mode[0, 0, 0, 1] + mode[2, 1, 0, 0])
        f[1, 0, 0, 1] = f[2, 0, 1, 0] = shear * (mode[1, 0, 0, 1] + mode[2, 0, 1, 0])
        for one, two in (
            ((0, 1, 1, 0), (2, 0, 1, 1)),
            ((0, 1, 0, 1), (1, 0, 1, 1)),
            ((1, 1, 1, 0), (2, 1, 0, 1)),
        ):
            f[one] = long3 * mode[one] + cross3 * mode[two]
            f[two] = long3 * mode[two] + cross3 * mode[one]
        twist = mode[0, 0, 1, 1] + mode[1, 1, 0, 1] + mode[2, 1, 1, 0]
        for key in ((0, 0, 1, 1), (1, 1, 0, 1), (2, 1, 1, 0)):
            f[key] = shear3 * (twist + mode[key])
        for comp in range(3):
            f[comp, 1, 1, 1] = long9 * mode[comp, 1, 1, 1]
        f = {key: value * scale for key, value in f.items()}
        for comp in range(3):
            for c in range(2):
                m01, m10, m11 = f[comp, 0, 1, c], f[comp, 1, 0, c], f[comp, 1, 1, c]
                total, other = m10 + m01, m10 - m01
                corners = (m11 - total, -m11 - other, other - m11, total + m11)
                if c == 1:
                    m00 = f[comp, 0, 0, 1]
                    corners = tuple(corner + m00 for corner in corners)
                for which in range(4):
                    corner_ref[8 * comp + 4 * c + which, pl.ds(at + 16, 8), :] = corners[which]

    shifts = (0, 1, 10, 11)
    for x in range(8):
        at = 10 * x + 11
        weight = sum(nodes_ref[4, pl.ds(at - shift, 8), :] for shift in shifts)
        below = jnp.where(first_lane, 0.0, pltpu.roll(weight, 1, 1))
        inverse = 1.0 / (0.125 * (weight + below))
        inverse_mass_ref[x] = inverse
        for comp in range(3):
            h0, h1 = (
                sum(
                    corner_ref[8 * comp + 4 * c + which, pl.ds(at + 16 - shift, 8), :]
                    for which, shift in enumerate(shifts)
                )
                for c in range(2)
            )
            below = jnp.where(first_lane, 0.0, pltpu.roll(h0 + h1, 1, 1))
            elastic = h0 - h1 + below
            velocity = velocity_ref[comp, x]
            acceleration = (load_ref[comp, x] - elastic) * inverse - DAMPING * velocity
            velocity = velocity + TIME_STEP * acceleration
            velocity_out_ref[comp, x] = velocity
            displacement_out_ref[comp, x] = u_ref[comp, x] + TIME_STEP * velocity


def spread_kernel(
    pulls_ref, depth_ref, weight_x_ref, weight_y_ref,
    velocity_ref, displacement_ref, inverse_mass_ref,
    displacement_out_ref, velocity_out_ref, terms_ref,
):
    for owner in range(32):
        weight_y = weight_y_ref[owner]
        planar = jnp.concatenate(
            [weight_y * weight_x_ref[x, pl.ds(owner, 1), :] for x in range(8)], axis=0
        )
        for comp in range(3):
            high, low = split(planar * pulls_ref[pl.ds(4 * owner + comp, 1), :])
            terms_ref[owner, pl.ds(64 * comp, 64), :] = high
            terms_ref[owner, pl.ds(192 + 64 * comp, 64), :] = low
    total = lax.dot_general(
        jnp.concatenate([terms_ref[owner] for owner in range(32)], axis=1),
        jnp.concatenate([depth_ref[owner] for owner in range(32)], axis=1),
        (((1,), (1,)), ((), ())),
        preferred_element_type=F32,
    )
    fibre = (total[:192, :LANES] + total[192:, :LANES]) + (
        total[:192, LANES:] + total[192:, LANES:]
    )
    for comp in range(3):
        for x in range(8):
            row = 64 * comp + 8 * x
            change = TIME_STEP * (fibre[row : row + 8] * inverse_mass_ref[x])
            velocity_out_ref[comp, x] = velocity_ref[comp, x] + change
            displacement_out_ref[comp, x] = displacement_ref[comp, x] + TIME_STEP * change


VMEM = pl.BlockSpec(memory_space=pltpu.VMEM)


def call(kernel, outs, ins, scratch=(), final=False, first=False):
    space = jax.ShapeDtypeStruct if final else pltpu.VMEM
    outs = tuple(space(shape, dtype) for shape, dtype in outs)
    space_in = pltpu.HBM if first else pltpu.VMEM
    ins = tuple(pltpu.with_memory_space_constraint(value, space_in) for value in ins)
    return pl.pallas_call(
        kernel,
        out_shape=outs,
        in_specs=[pl.BlockSpec(memory_space=space_in)] * len(ins),
        out_specs=(VMEM,) * len(outs),
        scratch_shapes=scratch,
        compiler_params=pltpu.CompilerParams(vmem_limit_bytes=16 << 20),
    )(*ins)


def swap(shard, axis, first):
    size = lax.axis_size(axis)
    pairs = [(i, i + 1) for i in range(first, size - 1, 2)]
    return lax.ppermute(shard, axis, pairs + [(b, a) for a, b in pairs])


def exchange(rows):
    blocks = rows.reshape(32, 4, LANES)
    blocks = lax.all_to_all(blocks, DOM, split_axis=0, concat_axis=0, tiled=True)
    return blocks.reshape(128, LANES)


def step(
    displacement, velocity, load, density, block_class,
    host_element, host_coords, fibre_slot, fibre_angles, fibre_stiffness,
):
    grid = (3, 8, 8, LANES)
    plane = (8, 8, LANES)
    side = ((50, LANES), F32)
    arguments = (
        displacement,
        host_element.reshape(32, LANES),
        host_coords.reshape(3, 32, LANES),
        density,
        block_class.reshape(1, 16),
        velocity,
        load,
        fibre_slot.reshape(16, LANES),
        fibre_angles.reshape(2, 16, LANES),
        fibre_stiffness.reshape(1, 16),
    )
    places, modulus, even_y, odd_y, weight_x, weight_y, *arguments = call(
        interpolate_kernel,
        (
            ((128, LANES), F32), (plane, F32), ((5, 8, LANES), F32), ((5, 8, LANES), F32),
            ((8, 32, LANES), F32), ((32, 8, LANES), F32),
        )
        + tuple((value.shape, value.dtype) for value in arguments),
        arguments,
        scratch=(pltpu.SemaphoreType.DMA((len(arguments),)),),
        first=True,
    )
    displacement, element, coords, density, _, velocity, load, slots, angles, stiffness = arguments
    even_y = swap(even_y, "blk", 0)
    odd_y = swap(odd_y, "blk", 1)
    received = exchange(places)
    table = ((32, LANES), jnp.int32)
    direction, stiff, fibre, node = call(
        fibre_tables_kernel,
        (((3, 16, LANES), F32), ((16, LANES), F32), table, table),
        (slots, angles, stiffness),
    )
    even_x, odd_x = call(
        sides_kernel, (side, side), (displacement, density, modulus, even_y, odd_y)
    )
    even_x = swap(even_x, DOM, 0)
    odd_x = swap(odd_x, DOM, 1)
    (pulls,) = call(
        fibre_kernel, (((128, LANES), F32),),
        (received, slots, direction, stiff, fibre, node),
    )
    returned = exchange(pulls)
    (depth,) = call(weights_kernel, (((32, 256, LANES), BF16),), (element, coords))
    new_velocity, new_displacement, inverse_mass = call(
        elastic_kernel,
        ((grid, F32), (grid, F32), (plane, F32)),
        (
            displacement, velocity, load, density, modulus,
            even_x, odd_x, even_y, odd_y,
        ),
        scratch=(
            pltpu.VMEM((5, ROWS_PAD, LANES), F32),
            pltpu.VMEM((6, ROWS_PAD, LANES), F32),
            pltpu.VMEM((24, ROWS_PAD, LANES), F32),
        ),
    )
    return call(
        spread_kernel, ((grid, F32), (grid, F32)),
        (returned, depth, weight_x, weight_y, new_velocity, new_displacement, inverse_mass),
        scratch=(pltpu.VMEM((32, 384, LANES), BF16),),
        final=True,
    )


def solution(mesh):
    finer = Mesh(
        mesh.devices.reshape(4, 4, 2, mesh.shape["blk"]), ("dom_0", "dom_1", "dom_2", "blk")
    )
    in_specs = (
        P(None, DOM, "blk", None),
        P(None, DOM, "blk", None),
        P(None, DOM, "blk", None),
        P(DOM, "blk", None),
        P(DOM, "blk", None),
        P("blk", DOM),
        P(None, "blk", DOM),
        P(DOM, "blk", None),
        P(None, DOM, "blk", None),
        P(DOM, "blk"),
    )
    out_specs = (P(None, DOM, "blk", None), P(None, DOM, "blk", None))
    return jax.shard_map(step, mesh=finer, in_specs=in_specs, out_specs=out_specs, check_vma=False)
```

```python
import jax
import jax.numpy as jnp
from jax import lax
from jax.experimental import pallas as pl
from jax.experimental.pallas import tpu as pltpu
from jax.sharding import Mesh
from jax.sharding import PartitionSpec as P

DOM = ("dom_0", "dom_1", "dom_2")
CLASS_VALUES = (1.0, 0.45, 0.12)
TIME_STEP = 0.25
DAMPING = 0.5
LAME = 0.3 / (1.3 * 0.4)
SHEAR = 0.5 / 1.3

F32 = jnp.float32
BF16 = jnp.bfloat16
LANES = 128
ROWS = 104
ROWS_PAD = 120


def odd_dom_index():
    return lax.axis_index("dom_2") == 1


def odd_blk_index():
    return (lax.axis_index("blk") & 1) == 1


def split(value):
    high = value.astype(BF16)
    low = (value - high.astype(F32)).astype(BF16)
    return high, low


def iota(shape, axis):
    return lax.broadcasted_iota(jnp.int32, shape, axis)


def hat(lowest, along, count):
    where = iota((count, LANES), 0)
    return jnp.where(
        where == lowest, 1.0 - along, jnp.where(where == lowest + 1, along, 0.0)
    )


def depth_weights(element, along):
    shape = (LANES, LANES)
    lowest = jnp.broadcast_to(element & (LANES - 1), shape).astype(jnp.int16)
    where = lax.broadcasted_iota(jnp.int16, shape, 0)
    here, above = where == lowest, where == lowest + jnp.int16(1)
    zero = jnp.zeros(shape, BF16)
    parts = []
    for lower, upper in zip(split(1.0 - along), split(along)):
        lower = jnp.broadcast_to(lower.astype(F32), shape).astype(BF16)
        upper = jnp.broadcast_to(upper.astype(F32), shape).astype(BF16)
        parts.append(jnp.where(here, lower, jnp.where(above, upper, zero)))
    return parts


def interpolate_kernel(*refs):
    count = (len(refs) - 7) // 2
    sources, targets, semaphores = refs[:count], refs[count + 6 : -1], refs[-1]
    places_ref, modulus_ref, even_ref, odd_ref, weight_x_ref, weight_y_ref = refs[
        count : count + 6
    ]
    copies = [
        pltpu.make_async_copy(source, target, semaphores.at[index])
        for index, (source, target) in enumerate(zip(sources, targets))
    ]
    for copy in copies:
        copy.start()
    u_ref, element_ref, coords_ref, density_ref, class_ref = targets[:5]
    for copy in copies[:5]:
        copy.wait()
    lowest, along = element_ref[...] >> 10, coords_ref[0]
    for x in range(8):
        weight_x_ref[x] = jnp.where(
            lowest == x, 1.0 - along, jnp.where(lowest == x - 1, along, 0.0)
        )
    field_high, field_low = split(u_ref[...].reshape(192, LANES))
    field = jnp.concatenate([field_high, field_low, field_high], axis=1)
    for pair in range(16):
        parts = []
        for owner in (2 * pair, 2 * pair + 1):
            row = pl.ds(owner, 1)
            high, low = depth_weights(element_ref[row, :], coords_ref[2, row, :])
            parts.append(jnp.concatenate([high, high, low], axis=0))
        sums = jnp.dot(field, jnp.concatenate(parts, axis=1), preferred_element_type=F32)
        for half in range(2):
            owner = 2 * pair + half
            row = pl.ds(owner, 1)
            weight_y = hat((element_ref[row, :] >> 7) & 7, coords_ref[1, row, :], 8)
            weight_y_ref[owner] = weight_y
            rows = [weight_x_ref[x, row, :] for x in range(8)]
            for comp in range(3):
                total = sum(
                    sums[64 * comp + 8 * x :, LANES * half : LANES * half + LANES][:8] * rows[x]
                    for x in range(8)
                )
                places_ref[pl.ds(4 * owner + comp, 1), :] = jnp.sum(
                    total * weight_y, axis=0, keepdims=True
                )
            places_ref[pl.ds(4 * owner + 3, 1), :] = jnp.zeros((1, LANES), F32)

    lane_block = iota((16, LANES), 1) >> 3
    pick = (lane_block == iota((16, LANES), 0)).astype(F32)
    kind = jnp.dot(
        jnp.broadcast_to(class_ref[...].astype(F32), (8, 16)), pick, preferred_element_type=F32
    )
    factor = jnp.zeros((8, LANES), F32)
    for index, value in enumerate(CLASS_VALUES):
        factor = factor + jnp.where(kind == float(index), value, 0.0)
    density = density_ref[...]
    modulus_ref[...] = factor[None] * density * density
    odd_dom = odd_dom_index()
    for comp in range(5):
        source = modulus_ref if comp == 3 else density_ref if comp == 4 else u_ref.at[comp]
        first, last = source[0], source[7]
        even_ref[comp] = jnp.where(odd_dom, first, last)
        odd_ref[comp] = jnp.where(odd_dom, last, first)
    for copy in copies[5:]:
        copy.wait()


def weights_kernel(element_ref, coords_ref, depth_ref):
    for owner in range(32):
        row = pl.ds(owner, 1)
        high, low = depth_weights(element_ref[row, :], coords_ref[2, row, :])
        depth_ref[owner, pl.ds(0, LANES), :] = high
        depth_ref[owner, pl.ds(LANES, LANES), :] = low


def fibre_tables_kernel(
    slots_ref, angles_ref, stiffness_ref, direction_ref, stiff_ref, fibre_ref, node_ref
):
    square = iota((16, 16), 0) == iota((16, 16), 1)
    stiffness = jnp.sum(jnp.where(square, stiffness_ref[...], 0.0), axis=1, keepdims=True)
    stiff_ref[...] = jnp.where(iota((16, LANES), 1) < LANES - 1, stiffness, 0.0)
    azimuth, elevation = angles_ref[0], angles_ref[1]
    flat = jnp.cos(elevation)
    direction_ref[0] = jnp.cos(azimuth) * flat
    direction_ref[1] = jnp.sin(azimuth) * flat
    direction_ref[2] = jnp.sin(elevation)
    lefts, rights = [], []
    nodes = iota((1, LANES), 1).astype(F32)
    for fibre in range(16):
        slots = slots_ref[pl.ds(fibre, 1), :]
        host = iota((32, LANES), 0) == (slots >> 7)
        lefts.append(
            jnp.concatenate(
                [jnp.where(host, float(fibre + 1), 0.0), jnp.where(host, nodes, 0.0)], axis=0
            ).astype(BF16)
        )
        rights.append((iota((LANES, LANES), 0) == (slots & 127)).astype(F32).astype(BF16))
    table = lax.dot_general(
        jnp.concatenate(lefts, axis=1),
        jnp.concatenate(rights, axis=1),
        (((1,), (1,)), ((), ())),
        preferred_element_type=F32,
    )
    table = table.astype(jnp.int32)
    fibre_ref[...] = table[:32]
    node_ref[...] = table[32:]


def lane_pick(row, index):
    return jnp.take_along_axis(jnp.broadcast_to(row, index.shape), index, axis=1)


def fibre_kernel(
    places_ref, slots_ref, direction_ref, stiff_ref, fibre_ref, node_ref, pulls_ref
):
    slots = slots_ref[...]
    host, spot = slots >> 7, slots & 127
    places = [jnp.zeros(slots.shape, F32) for _ in range(3)]
    for step in range(32):
        here = host == step
        for comp in range(3):
            picked = lane_pick(places_ref[pl.ds(4 * step + comp, 1), :], spot)
            places[comp] = jnp.where(here, picked, places[comp])
    strain = jnp.zeros(slots.shape, F32)
    for comp in range(3):
        ahead = pltpu.roll(places[comp], LANES - 1, 1)
        strain = strain + direction_ref[comp] * (ahead - places[comp])
    tension = stiff_ref[...] * jnp.maximum(strain, 0.0)
    forces = []
    for comp in range(3):
        pull = tension * direction_ref[comp]
        forces.append(pull - pltpu.roll(pull, 1, 1))
    for block in range(4):
        fibre = fibre_ref[pl.ds(8 * block, 8), :]
        node = node_ref[pl.ds(8 * block, 8), :]
        placed = [jnp.zeros((8, LANES), F32) for _ in range(3)]
        for step in range(16):
            here = fibre == step + 1
            for comp in range(3):
                picked = lane_pick(forces[comp][step : step + 1], node)
                placed[comp] = jnp.where(here, picked, placed[comp])
        for comp in range(3):
            pulls_ref[pl.ds(32 * block + comp, 8, stride=4), :] = placed[comp]
        pulls_ref[pl.ds(32 * block + 3, 8, stride=4), :] = jnp.zeros((8, LANES), F32)


def sides_kernel(
    u_ref, density_ref, modulus_ref, even_in_ref, odd_in_ref, even_ref, odd_swap_ref
):
    odd_dom = odd_dom_index()
    odd_blk = odd_blk_index()
    for comp in range(5):
        lower = jnp.where(odd_dom, even_in_ref[comp], odd_in_ref[comp])
        upper = jnp.where(odd_dom, odd_in_ref[comp], even_in_ref[comp])
        rows = []
        for at in (0, 7):
            if comp < 3:
                own = u_ref[comp, :, at, :]
            else:
                own = (modulus_ref if comp == 3 else density_ref)[:, at, :]
            rows.append(
                jnp.concatenate([lower[at : at + 1], own, upper[at : at + 1]], axis=0)
            )
        first, last = rows
        even_ref[pl.ds(10 * comp, 10), :] = jnp.where(odd_blk, first, last)
        odd_swap_ref[pl.ds(10 * comp, 10), :] = jnp.where(odd_blk, last, first)


def elastic_kernel(
    u_ref, velocity_ref, load_ref, density_ref, modulus_ref,
    even_x_ref, odd_x_ref, even_y_ref, odd_y_ref,
    velocity_out_ref, displacement_out_ref, inverse_mass_ref,
    nodes_ref, depth_ref, corner_ref,
):
    odd_dom = odd_dom_index()
    odd_blk = odd_blk_index()
    for comp in range(5):
        nodes_ref[comp, pl.ds(96, 24), :] = jnp.zeros((24, LANES), F32)
        lower = jnp.where(odd_dom, even_x_ref[comp], odd_x_ref[comp])
        upper = jnp.where(odd_dom, odd_x_ref[comp], even_x_ref[comp])
        nodes_ref[comp, pl.ds(1, 8), :] = lower
        nodes_ref[comp, pl.ds(91, 8), :] = upper
        for x in range(8):
            if comp < 3:
                own = u_ref[comp, x]
            else:
                own = (modulus_ref if comp == 3 else density_ref)[x]
            nodes_ref[comp, pl.ds(10 * x + 11, 8), :] = own
        even = even_y_ref[pl.ds(10 * comp, 10), :]
        odd = odd_y_ref[pl.ds(10 * comp, 10), :]
        left = jnp.where(odd_blk, even, odd)
        right = jnp.where(odd_blk, odd, even)
        for x in range(10):
            nodes_ref[comp, pl.ds(10 * x, 1), :] = left[x : x + 1]
            nodes_ref[comp, pl.ds(10 * x + 9, 1), :] = right[x : x + 1]
    last_lane = iota((8, LANES), 1) == LANES - 1
    first_lane = iota((8, LANES), 1) == 0
    for comp in range(3):
        for chunk in range(ROWS_PAD // 8):
            here = nodes_ref[comp, pl.ds(8 * chunk, 8), :]
            above = jnp.where(last_lane, 0.0, pltpu.roll(here, LANES - 1, 1))
            depth_ref[2 * comp, pl.ds(8 * chunk, 8), :] = above + here
            depth_ref[2 * comp + 1, pl.ds(8 * chunk, 8), :] = above - here

    long, cross, shear = (LAME + 2 * SHEAR) / 16, LAME / 16, SHEAR / 16
    long3, cross3, shear3 = (LAME + 3 * SHEAR) / 48, LAME / 48, SHEAR / 48
    long9 = (LAME + 4 * SHEAR) / 144
    for chunk in range(ROWS // 8):
        at = 8 * chunk
        mode = {}
        for comp in range(3):
            for c in range(2):
                a00 = depth_ref[2 * comp + c, pl.ds(at, 8), :]
                a01 = depth_ref[2 * comp + c, pl.ds(at + 1, 8), :]
                a10 = depth_ref[2 * comp + c, pl.ds(at + 10, 8), :]
                a11 = depth_ref[2 * comp + c, pl.ds(at + 11, 8), :]
                s0, d0, s1, d1 = a00 + a01, a01 - a00, a10 + a11, a11 - a10
                mode[comp, 0, 0, c] = s0 + s1
                mode[comp, 0, 1, c] = d0 + d1
                mode[comp, 1, 0, c] = s1 - s0
                mode[comp, 1, 1, c] = d1 - d0
        scale = nodes_ref[3, pl.ds(at, 8), :]
        u100, v010, w001 = mode[0, 1, 0, 0], mode[1, 0, 1, 0], mode[2, 0, 0, 1]
        trace = cross * (u100 + v010 + w001)
        f = {}
        f[0, 1, 0, 0] = (long - cross) * u100 + trace
        f[1, 0, 1, 0] = (long - cross) * v010 + trace
        f[2, 0, 0, 1] = (long - cross) * w001 + trace
        f[0, 0, 1, 0] = f[1, 1, 0, 0] = shear * (mode[0, 0, 1, 0] + mode[1, 1, 0, 0])
        f[0, 0, 0, 1] = f[2, 1, 0, 0] = shear * (mode[0, 0, 0, 1] + mode[2, 1, 0, 0])
        f[1, 0, 0, 1] = f[2, 0, 1, 0] = shear * (mode[1, 0, 0, 1] + mode[2, 0, 1, 0])
        for one, two in (
            ((0, 1, 1, 0), (2, 0, 1, 1)),
            ((0, 1, 0, 1), (1, 0, 1, 1)),
            ((1, 1, 1, 0), (2, 1, 0, 1)),
        ):
            f[one] = long3 * mode[one] + cross3 * mode[two]
            f[two] = long3 * mode[two] + cross3 * mode[one]
        twist = mode[0, 0, 1, 1] + mode[1, 1, 0, 1] + mode[2, 1, 1, 0]
        for key in ((0, 0, 1, 1), (1, 1, 0, 1), (2, 1, 1, 0)):
            f[key] = shear3 * (twist + mode[key])
        for comp in range(3):
            f[comp, 1, 1, 1] = long9 * mode[comp, 1, 1, 1]
        f = {key: value * scale for key, value in f.items()}
        for comp in range(3):
            for c in range(2):
                m01, m10, m11 = f[comp, 0, 1, c], f[comp, 1, 0, c], f[comp, 1, 1, c]
                total, other = m10 + m01, m10 - m01
                corners = (m11 - total, -m11 - other, other - m11, total + m11)
                if c == 1:
                    m00 = f[comp, 0, 0, 1]
                    corners = tuple(corner + m00 for corner in corners)
                for which in range(4):
                    corner_ref[8 * comp + 4 * c + which, pl.ds(at + 16, 8), :] = corners[which]

    shifts = (0, 1, 10, 11)
    for x in range(8):
        at = 10 * x + 11
        weight = sum(nodes_ref[4, pl.ds(at - shift, 8), :] for shift in shifts)
        below = jnp.where(first_lane, 0.0, pltpu.roll(weight, 1, 1))
        inverse = 1.0 / (0.125 * (weight + below))
        inverse_mass_ref[x] = inverse
        for comp in range(3):
            h0, h1 = (
                sum(
                    corner_ref[8 * comp + 4 * c + which, pl.ds(at + 16 - shift, 8), :]
                    for which, shift in enumerate(shifts)
                )
                for c in range(2)
            )
            below = jnp.where(first_lane, 0.0, pltpu.roll(h0 + h1, 1, 1))
            elastic = h0 - h1 + below
            velocity = velocity_ref[comp, x]
            acceleration = (load_ref[comp, x] - elastic) * inverse - DAMPING * velocity
            velocity = velocity + TIME_STEP * acceleration
            velocity_out_ref[comp, x] = velocity
            displacement_out_ref[comp, x] = u_ref[comp, x] + TIME_STEP * velocity


def spread_kernel(
    pulls_ref, depth_ref, weight_x_ref, weight_y_ref,
    velocity_ref, displacement_ref, inverse_mass_ref,
    displacement_out_ref, velocity_out_ref, terms_ref,
):
    for owner in range(32):
        weight_y = weight_y_ref[owner]
        planar = jnp.concatenate(
            [weight_y * weight_x_ref[x, pl.ds(owner, 1), :] for x in range(8)], axis=0
        )
        for comp in range(3):
            high, low = split(planar * pulls_ref[pl.ds(4 * owner + comp, 1), :])
            terms_ref[owner, pl.ds(64 * comp, 64), :] = high
            terms_ref[owner, pl.ds(192 + 64 * comp, 64), :] = low
    total = lax.dot_general(
        jnp.concatenate([terms_ref[owner] for owner in range(32)], axis=1),
        jnp.concatenate([depth_ref[owner] for owner in range(32)], axis=1),
        (((1,), (1,)), ((), ())),
        preferred_element_type=F32,
    )
    fibre = (total[:192, :LANES] + total[192:, :LANES]) + (
        total[:192, LANES:] + total[192:, LANES:]
    )
    for comp in range(3):
        for x in range(8):
            row = 64 * comp + 8 * x
            change = TIME_STEP * (fibre[row : row + 8] * inverse_mass_ref[x])
            velocity_out_ref[comp, x] = velocity_ref[comp, x] + change
            displacement_out_ref[comp, x] = displacement_ref[comp, x] + TIME_STEP * change


VMEM = pl.BlockSpec(memory_space=pltpu.VMEM)


def call(kernel, outs, ins, scratch=(), final=False, first=False):
    space = jax.ShapeDtypeStruct if final else pltpu.VMEM
    outs = tuple(space(shape, dtype) for shape, dtype in outs)
    space_in = pltpu.HBM if first else pltpu.VMEM
    ins = tuple(pltpu.with_memory_space_constraint(value, space_in) for value in ins)
    return pl.pallas_call(
        kernel,
        out_shape=outs,
        in_specs=[pl.BlockSpec(memory_space=space_in)] * len(ins),
        out_specs=(VMEM,) * len(outs),
        scratch_shapes=scratch,
        compiler_params=pltpu.CompilerParams(vmem_limit_bytes=16 << 20),
    )(*ins)


def swap(shard, axis, first):
    size = lax.axis_size(axis)
    pairs = [(i, i + 1) for i in range(first, size - 1, 2)]
    return lax.ppermute(shard, axis, pairs + [(b, a) for a, b in pairs])


def exchange(rows):
    blocks = rows.reshape(32, 4, LANES)
    blocks = lax.all_to_all(blocks, DOM, split_axis=0, concat_axis=0, tiled=True)
    return blocks.reshape(128, LANES)


def step(
    displacement, velocity, load, density, block_class,
    host_element, host_coords, fibre_slot, fibre_angles, fibre_stiffness,
):
    grid = (3, 8, 8, LANES)
    plane = (8, 8, LANES)
    side = ((50, LANES), F32)
    arguments = (
        displacement,
        host_element.reshape(32, LANES),
        host_coords.reshape(3, 32, LANES),
        density,
        block_class.reshape(1, 16),
        velocity,
        load,
        fibre_slot.reshape(16, LANES),
        fibre_angles.reshape(2, 16, LANES),
        fibre_stiffness.reshape(1, 16),
    )
    places, modulus, even_x, odd_x, weight_x, weight_y, *arguments = call(
        interpolate_kernel,
        (
            ((128, LANES), F32), (plane, F32), ((5, 8, LANES), F32), ((5, 8, LANES), F32),
            ((8, 32, LANES), F32), ((32, 8, LANES), F32),
        )
        + tuple((value.shape, value.dtype) for value in arguments),
        arguments,
        scratch=(pltpu.SemaphoreType.DMA((len(arguments),)),),
        first=True,
    )
    displacement, element, coords, density, _, velocity, load, slots, angles, stiffness = arguments
    even_x = swap(even_x, DOM, 0)
    odd_x = swap(odd_x, DOM, 1)
    received = exchange(places)
    table = ((32, LANES), jnp.int32)
    direction, stiff, fibre, node = call(
        fibre_tables_kernel,
        (((3, 16, LANES), F32), ((16, LANES), F32), table, table),
        (slots, angles, stiffness),
    )
    even_y, odd_y = call(
        sides_kernel, (side, side), (displacement, density, modulus, even_x, odd_x)
    )
    even_y = swap(even_y, "blk", 0)
    odd_y = swap(odd_y, "blk", 1)
    (pulls,) = call(
        fibre_kernel, (((128, LANES), F32),),
        (received, slots, direction, stiff, fibre, node),
    )
    returned = exchange(pulls)
    (depth,) = call(weights_kernel, (((32, 256, LANES), BF16),), (element, coords))
    new_velocity, new_displacement, inverse_mass = call(
        elastic_kernel,
        ((grid, F32), (grid, F32), (plane, F32)),
        (
            displacement, velocity, load, density, modulus,
            even_x, odd_x, even_y, odd_y,
        ),
        scratch=(
            pltpu.VMEM((5, ROWS_PAD, LANES), F32),
            pltpu.VMEM((6, ROWS_PAD, LANES), F32),
            pltpu.VMEM((24, ROWS_PAD, LANES), F32),
        ),
    )
    return call(
        spread_kernel, ((grid, F32), (grid, F32)),
        (returned, depth, weight_x, weight_y, new_velocity, new_displacement, inverse_mass),
        scratch=(pltpu.VMEM((32, 384, LANES), BF16),),
        final=True,
    )


def solution(mesh):
    finer = Mesh(
        mesh.devices.reshape(4, 4, 2, mesh.shape["blk"]), ("dom_0", "dom_1", "dom_2", "blk")
    )
    in_specs = (
        P(None, DOM, "blk", None),
        P(None, DOM, "blk", None),
        P(None, DOM, "blk", None),
        P(DOM, "blk", None),
        P(DOM, "blk", None),
        P("blk", DOM),
        P(None, "blk", DOM),
        P(DOM, "blk", None),
        P(None, DOM, "blk", None),
        P(DOM, "blk"),
    )
    out_specs = (P(None, DOM, "blk", None), P(None, DOM, "blk", None))
    return jax.shard_map(step, mesh=finer, in_specs=in_specs, out_specs=out_specs, check_vma=False)
```

```python
import jax
import jax.numpy as jnp
from jax import lax
from jax.experimental import pallas as pl
from jax.experimental.pallas import tpu as pltpu
from jax.sharding import Mesh
from jax.sharding import PartitionSpec as P

DOM = ("dom_0", "dom_1", "dom_2")
CLASS_VALUES = (1.0, 0.45, 0.12)
TIME_STEP = 0.25
DAMPING = 0.5
LAME = 0.3 / (1.3 * 0.4)
SHEAR = 0.5 / 1.3

F32 = jnp.float32
BF16 = jnp.bfloat16
LANES = 128
ROWS = 104
ROWS_PAD = 120


def odd_dom_index():
    return lax.axis_index("dom_2") == 1


def odd_blk_index():
    return (lax.axis_index("blk") & 1) == 1


def at_end(axis):
    axes = axis if isinstance(axis, tuple) else (axis,)
    index, size = 0, 1
    for name in axes:
        index = index * lax.axis_size(name) + lax.axis_index(name)
        size *= lax.axis_size(name)
    return (index == 0) | (index == size - 1)


def split(value):
    high = value.astype(BF16)
    low = (value - high.astype(F32)).astype(BF16)
    return high, low


def iota(shape, axis):
    return lax.broadcasted_iota(jnp.int32, shape, axis)


def hat(lowest, along, count):
    where = iota((count, LANES), 0)
    return jnp.where(
        where == lowest, 1.0 - along, jnp.where(where == lowest + 1, along, 0.0)
    )


def depth_weights(element, along):
    shape = (LANES, LANES)
    lowest = jnp.broadcast_to(element & (LANES - 1), shape).astype(jnp.int16)
    where = lax.broadcasted_iota(jnp.int16, shape, 0)
    here, above = where == lowest, where == lowest + jnp.int16(1)
    zero = jnp.zeros(shape, BF16)
    parts = []
    for lower, upper in zip(split(1.0 - along), split(along)):
        lower = jnp.broadcast_to(lower.astype(F32), shape).astype(BF16)
        upper = jnp.broadcast_to(upper.astype(F32), shape).astype(BF16)
        parts.append(jnp.where(here, lower, jnp.where(above, upper, zero)))
    return parts


def interpolate_kernel(*refs):
    count = (len(refs) - 7) // 2
    sources, targets, semaphores = refs[:count], refs[count + 6 : -1], refs[-1]
    places_ref, modulus_ref, even_ref, odd_ref, weight_x_ref, weight_y_ref = refs[
        count : count + 6
    ]
    copies = [
        pltpu.make_async_copy(source, target, semaphores.at[index])
        for index, (source, target) in enumerate(zip(sources, targets))
    ]
    for copy in copies:
        copy.start()
    u_ref, element_ref, coords_ref, density_ref, class_ref = targets[:5]
    for copy in copies[:5]:
        copy.wait()
    lowest, along = element_ref[...] >> 10, coords_ref[0]
    for x in range(8):
        weight_x_ref[x] = jnp.where(
            lowest == x, 1.0 - along, jnp.where(lowest == x - 1, along, 0.0)
        )
    field_high, field_low = split(u_ref[...].reshape(192, LANES))
    field = jnp.concatenate([field_high, field_low, field_high], axis=1)
    for pair in range(16):
        parts = []
        for owner in (2 * pair, 2 * pair + 1):
            row = pl.ds(owner, 1)
            high, low = depth_weights(element_ref[row, :], coords_ref[2, row, :])
            parts.append(jnp.concatenate([high, high, low], axis=0))
        sums = jnp.dot(field, jnp.concatenate(parts, axis=1), preferred_element_type=F32)
        for half in range(2):
            owner = 2 * pair + half
            row = pl.ds(owner, 1)
            weight_y = hat((element_ref[row, :] >> 7) & 7, coords_ref[1, row, :], 8)
            weight_y_ref[owner] = weight_y
            rows = [weight_x_ref[x, row, :] for x in range(8)]
            for comp in range(3):
                total = sum(
                    sums[64 * comp + 8 * x :, LANES * half : LANES * half + LANES][:8] * rows[x]
                    for x in range(8)
                )
                places_ref[pl.ds(4 * owner + comp, 1), :] = jnp.sum(
                    total * weight_y, axis=0, keepdims=True
                )
            places_ref[pl.ds(4 * owner + 3, 1), :] = jnp.zeros((1, LANES), F32)

    lane_block = iota((16, LANES), 1) >> 3
    pick = (lane_block == iota((16, LANES), 0)).astype(F32)
    kind = jnp.dot(
        jnp.broadcast_to(class_ref[...].astype(F32), (8, 16)), pick, preferred_element_type=F32
    )
    factor = jnp.zeros((8, LANES), F32)
    for index, value in enumerate(CLASS_VALUES):
        factor = factor + jnp.where(kind == float(index), value, 0.0)
    density = density_ref[...]
    modulus_ref[...] = factor[None] * density * density
    odd_dom, end = odd_dom_index(), at_end(DOM)
    for comp in range(5):
        source = modulus_ref if comp == 3 else density_ref if comp == 4 else u_ref.at[comp]
        first, last = source[0], source[7]
        even_ref[comp] = jnp.where(odd_dom, first, last)
        odd_ref[comp] = jnp.where(end, 0.0, jnp.where(odd_dom, last, first))
    for copy in copies[5:]:
        copy.wait()


def weights_kernel(element_ref, coords_ref, depth_ref):
    for owner in range(32):
        row = pl.ds(owner, 1)
        high, low = depth_weights(element_ref[row, :], coords_ref[2, row, :])
        depth_ref[owner, pl.ds(0, LANES), :] = high
        depth_ref[owner, pl.ds(LANES, LANES), :] = low


def fibre_tables_kernel(
    slots_ref, angles_ref, stiffness_ref, direction_ref, stiff_ref, fibre_ref, node_ref
):
    square = iota((16, 16), 0) == iota((16, 16), 1)
    stiffness = jnp.sum(jnp.where(square, stiffness_ref[...], 0.0), axis=1, keepdims=True)
    stiff_ref[...] = jnp.where(iota((16, LANES), 1) < LANES - 1, stiffness, 0.0)
    azimuth, elevation = angles_ref[0], angles_ref[1]
    flat = jnp.cos(elevation)
    direction_ref[0] = jnp.cos(azimuth) * flat
    direction_ref[1] = jnp.sin(azimuth) * flat
    direction_ref[2] = jnp.sin(elevation)
    lefts, rights = [], []
    nodes = iota((1, LANES), 1).astype(F32)
    for fibre in range(16):
        slots = slots_ref[pl.ds(fibre, 1), :]
        host = iota((32, LANES), 0) == (slots >> 7)
        lefts.append(
            jnp.concatenate(
                [jnp.where(host, float(fibre + 1), 0.0), jnp.where(host, nodes, 0.0)], axis=0
            ).astype(BF16)
        )
        rights.append((iota((LANES, LANES), 0) == (slots & 127)).astype(F32).astype(BF16))
    table = lax.dot_general(
        jnp.concatenate(lefts, axis=1),
        jnp.concatenate(rights, axis=1),
        (((1,), (1,)), ((), ())),
        preferred_element_type=F32,
    )
    table = table.astype(jnp.int32)
    fibre_ref[...] = table[:32]
    node_ref[...] = table[32:]


def lane_pick(row, index):
    return jnp.take_along_axis(jnp.broadcast_to(row, index.shape), index, axis=1)


def fibre_kernel(
    places_ref, slots_ref, direction_ref, stiff_ref, fibre_ref, node_ref, pulls_ref
):
    slots = slots_ref[...]
    host, spot = slots >> 7, slots & 127
    places = [jnp.zeros(slots.shape, F32) for _ in range(3)]
    for step in range(32):
        here = host == step
        for comp in range(3):
            picked = lane_pick(places_ref[pl.ds(4 * step + comp, 1), :], spot)
            places[comp] = jnp.where(here, picked, places[comp])
    strain = jnp.zeros(slots.shape, F32)
    for comp in range(3):
        ahead = pltpu.roll(places[comp], LANES - 1, 1)
        strain = strain + direction_ref[comp] * (ahead - places[comp])
    tension = stiff_ref[...] * jnp.maximum(strain, 0.0)
    forces = []
    for comp in range(3):
        pull = tension * direction_ref[comp]
        forces.append(pull - pltpu.roll(pull, 1, 1))
    for block in range(4):
        fibre = fibre_ref[pl.ds(8 * block, 8), :]
        node = node_ref[pl.ds(8 * block, 8), :]
        placed = [jnp.zeros((8, LANES), F32) for _ in range(3)]
        for step in range(16):
            here = fibre == step + 1
            for comp in range(3):
                picked = lane_pick(forces[comp][step : step + 1], node)
                placed[comp] = jnp.where(here, picked, placed[comp])
        for comp in range(3):
            pulls_ref[pl.ds(32 * block + comp, 8, stride=4), :] = placed[comp]
        pulls_ref[pl.ds(32 * block + 3, 8, stride=4), :] = jnp.zeros((8, LANES), F32)


def sides_kernel(
    u_ref, density_ref, modulus_ref, even_in_ref, odd_in_ref, even_ref, odd_swap_ref
):
    odd_dom = odd_dom_index()
    odd_blk, end = odd_blk_index(), at_end("blk")
    for comp in range(5):
        lower = jnp.where(odd_dom, even_in_ref[comp], odd_in_ref[comp])
        upper = jnp.where(odd_dom, odd_in_ref[comp], even_in_ref[comp])
        rows = []
        for at in (0, 7):
            if comp < 3:
                own = u_ref[comp, :, at, :]
            else:
                own = (modulus_ref if comp == 3 else density_ref)[:, at, :]
            rows.append(
                jnp.concatenate([lower[at : at + 1], own, upper[at : at + 1]], axis=0)
            )
        first, last = rows
        even_ref[pl.ds(10 * comp, 10), :] = jnp.where(odd_blk, first, last)
        odd_swap_ref[pl.ds(10 * comp, 10), :] = jnp.where(
            end, 0.0, jnp.where(odd_blk, last, first)
        )


def elastic_kernel(
    u_ref, velocity_ref, load_ref, density_ref, modulus_ref,
    even_x_ref, odd_x_ref, even_y_ref, odd_y_ref,
    velocity_out_ref, displacement_out_ref, inverse_mass_ref,
    nodes_ref, depth_ref, corner_ref,
):
    odd_dom = odd_dom_index()
    odd_blk = odd_blk_index()
    for comp in range(5):
        nodes_ref[comp, pl.ds(96, 24), :] = jnp.zeros((24, LANES), F32)
        lower = jnp.where(odd_dom, even_x_ref[comp], odd_x_ref[comp])
        upper = jnp.where(odd_dom, odd_x_ref[comp], even_x_ref[comp])
        nodes_ref[comp, pl.ds(1, 8), :] = lower
        nodes_ref[comp, pl.ds(91, 8), :] = upper
        for x in range(8):
            if comp < 3:
                own = u_ref[comp, x]
            else:
                own = (modulus_ref if comp == 3 else density_ref)[x]
            nodes_ref[comp, pl.ds(10 * x + 11, 8), :] = own
        even = even_y_ref[pl.ds(10 * comp, 10), :]
        odd = odd_y_ref[pl.ds(10 * comp, 10), :]
        left = jnp.where(odd_blk, even, odd)
        right = jnp.where(odd_blk, odd, even)
        for x in range(10):
            nodes_ref[comp, pl.ds(10 * x, 1), :] = left[x : x + 1]
            nodes_ref[comp, pl.ds(10 * x + 9, 1), :] = right[x : x + 1]
    last_lane = iota((8, LANES), 1) == LANES - 1
    first_lane = iota((8, LANES), 1) == 0
    for comp in range(3):
        for chunk in range(ROWS_PAD // 8):
            here = nodes_ref[comp, pl.ds(8 * chunk, 8), :]
            above = jnp.where(last_lane, 0.0, pltpu.roll(here, LANES - 1, 1))
            depth_ref[2 * comp, pl.ds(8 * chunk, 8), :] = above + here
            depth_ref[2 * comp + 1, pl.ds(8 * chunk, 8), :] = above - here

    long, cross, shear = (LAME + 2 * SHEAR) / 16, LAME / 16, SHEAR / 16
    long3, cross3, shear3 = (LAME + 3 * SHEAR) / 48, LAME / 48, SHEAR / 48
    long9 = (LAME + 4 * SHEAR) / 144
    for chunk in range(ROWS // 8):
        at = 8 * chunk
        mode = {}
        for comp in range(3):
            for c in range(2):
                a00 = depth_ref[2 * comp + c, pl.ds(at, 8), :]
                a01 = depth_ref[2 * comp + c, pl.ds(at + 1, 8), :]
                a10 = depth_ref[2 * comp + c, pl.ds(at + 10, 8), :]
                a11 = depth_ref[2 * comp + c, pl.ds(at + 11, 8), :]
                s0, d0, s1, d1 = a00 + a01, a01 - a00, a10 + a11, a11 - a10
                mode[comp, 0, 0, c] = s0 + s1
                mode[comp, 0, 1, c] = d0 + d1
                mode[comp, 1, 0, c] = s1 - s0
                mode[comp, 1, 1, c] = d1 - d0
        scale = nodes_ref[3, pl.ds(at, 8), :]
        u100, v010, w001 = mode[0, 1, 0, 0], mode[1, 0, 1, 0], mode[2, 0, 0, 1]
        trace = cross * (u100 + v010 + w001)
        f = {}
        f[0, 1, 0, 0] = (long - cross) * u100 + trace
        f[1, 0, 1, 0] = (long - cross) * v010 + trace
        f[2, 0, 0, 1] = (long - cross) * w001 + trace
        f[0, 0, 1, 0] = f[1, 1, 0, 0] = shear * (mode[0, 0, 1, 0] + mode[1, 1, 0, 0])
        f[0, 0, 0, 1] = f[2, 1, 0, 0] = shear * (mode[0, 0, 0, 1] + mode[2, 1, 0, 0])
        f[1, 0, 0, 1] = f[2, 0, 1, 0] = shear * (mode[1, 0, 0, 1] + mode[2, 0, 1, 0])
        for one, two in (
            ((0, 1, 1, 0), (2, 0, 1, 1)),
            ((0, 1, 0, 1), (1, 0, 1, 1)),
            ((1, 1, 1, 0), (2, 1, 0, 1)),
        ):
            f[one] = long3 * mode[one] + cross3 * mode[two]
            f[two] = long3 * mode[two] + cross3 * mode[one]
        twist = mode[0, 0, 1, 1] + mode[1, 1, 0, 1] + mode[2, 1, 1, 0]
        for key in ((0, 0, 1, 1), (1, 1, 0, 1), (2, 1, 1, 0)):
            f[key] = shear3 * (twist + mode[key])
        for comp in range(3):
            f[comp, 1, 1, 1] = long9 * mode[comp, 1, 1, 1]
        f = {key: value * scale for key, value in f.items()}
        for comp in range(3):
            for c in range(2):
                m01, m10, m11 = f[comp, 0, 1, c], f[comp, 1, 0, c], f[comp, 1, 1, c]
                total, other = m10 + m01, m10 - m01
                corners = (m11 - total, -m11 - other, other - m11, total + m11)
                if c == 1:
                    m00 = f[comp, 0, 0, 1]
                    corners = tuple(corner + m00 for corner in corners)
                for which in range(4):
                    corner_ref[8 * comp + 4 * c + which, pl.ds(at + 16, 8), :] = corners[which]

    shifts = (0, 1, 10, 11)
    for x in range(8):
        at = 10 * x + 11
        weight = sum(nodes_ref[4, pl.ds(at - shift, 8), :] for shift in shifts)
        below = jnp.where(first_lane, 0.0, pltpu.roll(weight, 1, 1))
        inverse = 1.0 / (0.125 * (weight + below))
        inverse_mass_ref[x] = inverse
        for comp in range(3):
            h0, h1 = (
                sum(
                    corner_ref[8 * comp + 4 * c + which, pl.ds(at + 16 - shift, 8), :]
                    for which, shift in enumerate(shifts)
                )
                for c in range(2)
            )
            below = jnp.where(first_lane, 0.0, pltpu.roll(h0 + h1, 1, 1))
            elastic = h0 - h1 + below
            velocity = velocity_ref[comp, x]
            acceleration = (load_ref[comp, x] - elastic) * inverse - DAMPING * velocity
            velocity = velocity + TIME_STEP * acceleration
            velocity_out_ref[comp, x] = velocity
            displacement_out_ref[comp, x] = u_ref[comp, x] + TIME_STEP * velocity


def spread_kernel(
    pulls_ref, depth_ref, weight_x_ref, weight_y_ref,
    velocity_ref, displacement_ref, inverse_mass_ref,
    displacement_out_ref, velocity_out_ref, terms_ref,
):
    for owner in range(32):
        weight_y = weight_y_ref[owner]
        planar = jnp.concatenate(
            [weight_y * weight_x_ref[x, pl.ds(owner, 1), :] for x in range(8)], axis=0
        )
        for comp in range(3):
            high, low = split(planar * pulls_ref[pl.ds(4 * owner + comp, 1), :])
            terms_ref[owner, pl.ds(64 * comp, 64), :] = high
            terms_ref[owner, pl.ds(192 + 64 * comp, 64), :] = low
    total = lax.dot_general(
        jnp.concatenate([terms_ref[owner] for owner in range(32)], axis=1),
        jnp.concatenate([depth_ref[owner] for owner in range(32)], axis=1),
        (((1,), (1,)), ((), ())),
        preferred_element_type=F32,
    )
    fibre = (total[:192, :LANES] + total[192:, :LANES]) + (
        total[:192, LANES:] + total[192:, LANES:]
    )
    for comp in range(3):
        for x in range(8):
            row = 64 * comp + 8 * x
            change = TIME_STEP * (fibre[row : row + 8] * inverse_mass_ref[x])
            velocity_out_ref[comp, x] = velocity_ref[comp, x] + change
            displacement_out_ref[comp, x] = displacement_ref[comp, x] + TIME_STEP * change


VMEM = pl.BlockSpec(memory_space=pltpu.VMEM)


def call(kernel, outs, ins, scratch=(), final=False, first=False):
    space = jax.ShapeDtypeStruct if final else pltpu.VMEM
    outs = tuple(space(shape, dtype) for shape, dtype in outs)
    space_in = pltpu.HBM if first else pltpu.VMEM
    ins = tuple(pltpu.with_memory_space_constraint(value, space_in) for value in ins)
    return pl.pallas_call(
        kernel,
        out_shape=outs,
        in_specs=[pl.BlockSpec(memory_space=space_in)] * len(ins),
        out_specs=(VMEM,) * len(outs),
        scratch_shapes=scratch,
        compiler_params=pltpu.CompilerParams(vmem_limit_bytes=16 << 20),
    )(*ins)


def swap(shard, axis, first):
    doms = lax.axis_size(DOM)
    blks = lax.axis_size("blk")
    pairs = []
    for dom in range(doms):
        for blk in range(blks):
            at, size = (blk, blks) if axis == "blk" else (dom, doms)
            low = (at - first) % 2 == 0
            move = 1 if low else -1
            along_blk = (axis == "blk") == (0 <= at + move < size)
            if not 0 <= at + move < size:
                move = 1 if (dom if axis == "blk" else blk) % 2 == 0 else -1
            target = (dom, blk + move) if along_blk else (dom + move, blk)
            pairs.append((dom * blks + blk, target[0] * blks + target[1]))
    return lax.ppermute(shard, (*DOM, "blk"), pairs)


def exchange(rows):
    blocks = rows.reshape(32, 4, LANES)
    blocks = lax.all_to_all(blocks, DOM, split_axis=0, concat_axis=0, tiled=True)
    return blocks.reshape(128, LANES)


def step(
    displacement, velocity, load, density, block_class,
    host_element, host_coords, fibre_slot, fibre_angles, fibre_stiffness,
):
    grid = (3, 8, 8, LANES)
    plane = (8, 8, LANES)
    side = ((50, LANES), F32)
    arguments = (
        displacement,
        host_element.reshape(32, LANES),
        host_coords.reshape(3, 32, LANES),
        density,
        block_class.reshape(1, 16),
        velocity,
        load,
        fibre_slot.reshape(16, LANES),
        fibre_angles.reshape(2, 16, LANES),
        fibre_stiffness.reshape(1, 16),
    )
    places, modulus, even_x, odd_x, weight_x, weight_y, *arguments = call(
        interpolate_kernel,
        (
            ((128, LANES), F32), (plane, F32), ((5, 8, LANES), F32), ((5, 8, LANES), F32),
            ((8, 32, LANES), F32), ((32, 8, LANES), F32),
        )
        + tuple((value.shape, value.dtype) for value in arguments),
        arguments,
        scratch=(pltpu.SemaphoreType.DMA((len(arguments),)),),
        first=True,
    )
    displacement, element, coords, density, _, velocity, load, slots, angles, stiffness = arguments
    even_x = swap(even_x, DOM, 0)
    odd_x = swap(odd_x, DOM, 1)
    received = exchange(places)
    table = ((32, LANES), jnp.int32)
    direction, stiff, fibre, node = call(
        fibre_tables_kernel,
        (((3, 16, LANES), F32), ((16, LANES), F32), table, table),
        (slots, angles, stiffness),
    )
    even_y, odd_y = call(
        sides_kernel, (side, side), (displacement, density, modulus, even_x, odd_x)
    )
    even_y = swap(even_y, "blk", 0)
    odd_y = swap(odd_y, "blk", 1)
    (pulls,) = call(
        fibre_kernel, (((128, LANES), F32),),
        (received, slots, direction, stiff, fibre, node),
    )
    returned = exchange(pulls)
    (depth,) = call(weights_kernel, (((32, 256, LANES), BF16),), (element, coords))
    new_velocity, new_displacement, inverse_mass = call(
        elastic_kernel,
        ((grid, F32), (grid, F32), (plane, F32)),
        (
            displacement, velocity, load, density, modulus,
            even_x, odd_x, even_y, odd_y,
        ),
        scratch=(
            pltpu.VMEM((5, ROWS_PAD, LANES), F32),
            pltpu.VMEM((6, ROWS_PAD, LANES), F32),
            pltpu.VMEM((24, ROWS_PAD, LANES), F32),
        ),
    )
    return call(
        spread_kernel, ((grid, F32), (grid, F32)),
        (returned, depth, weight_x, weight_y, new_velocity, new_displacement, inverse_mass),
        scratch=(pltpu.VMEM((32, 384, LANES), BF16),),
        final=True,
    )


def solution(mesh):
    finer = Mesh(
        mesh.devices.reshape(4, 4, 2, mesh.shape["blk"]), ("dom_0", "dom_1", "dom_2", "blk")
    )
    in_specs = (
        P(None, DOM, "blk", None),
        P(None, DOM, "blk", None),
        P(None, DOM, "blk", None),
        P(DOM, "blk", None),
        P(DOM, "blk", None),
        P("blk", DOM),
        P(None, "blk", DOM),
        P(DOM, "blk", None),
        P(None, DOM, "blk", None),
        P(DOM, "blk"),
    )
    out_specs = (P(None, DOM, "blk", None), P(None, DOM, "blk", None))
    return jax.shard_map(step, mesh=finer, in_specs=in_specs, out_specs=out_specs, check_vma=False)
```

```python
import jax
import jax.numpy as jnp
from jax import lax
from jax.experimental import pallas as pl
from jax.experimental.pallas import tpu as pltpu
from jax.sharding import Mesh
from jax.sharding import PartitionSpec as P

DOM = ("dom_0", "dom_1", "dom_2")
CLASS_VALUES = (1.0, 0.45, 0.12)
TIME_STEP = 0.25
DAMPING = 0.5
LAME = 0.3 / (1.3 * 0.4)
SHEAR = 0.5 / 1.3

F32 = jnp.float32
BF16 = jnp.bfloat16
LANES = 128
GATHERED = (2, 5, 8, 11, 14)
ROWS = 104
ROWS_PAD = 120


def odd_dom_index():
    return lax.axis_index("dom_2") == 1


def odd_blk_index():
    return (lax.axis_index("blk") & 1) == 1


def at_end(axis):
    axes = axis if isinstance(axis, tuple) else (axis,)
    index, size = 0, 1
    for name in axes:
        index = index * lax.axis_size(name) + lax.axis_index(name)
        size *= lax.axis_size(name)
    return (index == 0) | (index == size - 1)


def split(value):
    high = value.astype(BF16)
    low = (value - high.astype(F32)).astype(BF16)
    return high, low


def iota(shape, axis):
    return lax.broadcasted_iota(jnp.int32, shape, axis)


def hat(lowest, along, count):
    where = iota((count, LANES), 0)
    return jnp.where(
        where == lowest, 1.0 - along, jnp.where(where == lowest + 1, along, 0.0)
    )


def depth_weights(element, along):
    shape = (LANES, LANES)
    lowest = jnp.broadcast_to(element & (LANES - 1), shape).astype(jnp.int16)
    where = lax.broadcasted_iota(jnp.int16, shape, 0)
    here, above = where == lowest, where == lowest + jnp.int16(1)
    zero = jnp.zeros(shape, BF16)
    parts = []
    for lower, upper in zip(split(1.0 - along), split(along)):
        lower = jnp.broadcast_to(lower.astype(F32), shape).astype(BF16)
        upper = jnp.broadcast_to(upper.astype(F32), shape).astype(BF16)
        parts.append(jnp.where(here, lower, jnp.where(above, upper, zero)))
    return parts


def gathered(field_ref, index, rows):
    return [
        sum(
            jnp.take_along_axis(field_ref[comp, x], index, axis=1) * rows[x] for x in range(8)
        )
        for comp in range(3)
    ]


def interpolate_kernel(*refs):
    count = (len(refs) - 7) // 2
    sources, targets, semaphores = refs[:count], refs[count + 6 : -1], refs[-1]
    places_ref, modulus_ref, even_ref, odd_ref, weight_x_ref, weight_y_ref = refs[
        count : count + 6
    ]
    copies = [
        pltpu.make_async_copy(source, target, semaphores.at[index])
        for index, (source, target) in enumerate(zip(sources, targets))
    ]
    for copy in copies:
        copy.start()
    u_ref, element_ref, coords_ref, density_ref, class_ref = targets[:5]
    for copy in copies[:5]:
        copy.wait()
    lowest, along = element_ref[...] >> 10, coords_ref[0]
    for x in range(8):
        weight_x_ref[x] = jnp.where(
            lowest == x, 1.0 - along, jnp.where(lowest == x - 1, along, 0.0)
        )
    field_high, field_low = split(u_ref[...].reshape(192, LANES))
    field = jnp.concatenate([field_high, field_low, field_high], axis=1)
    for pair in range(16):
        by_gather = pair in GATHERED
        if not by_gather:
            parts = []
            for owner in (2 * pair, 2 * pair + 1):
                row = pl.ds(owner, 1)
                high, low = depth_weights(element_ref[row, :], coords_ref[2, row, :])
                parts.append(jnp.concatenate([high, high, low], axis=0))
            sums = jnp.dot(field, jnp.concatenate(parts, axis=1), preferred_element_type=F32)
        for half in range(2):
            owner = 2 * pair + half
            row = pl.ds(owner, 1)
            element = element_ref[row, :]
            weight_y = hat((element >> 7) & 7, coords_ref[1, row, :], 8)
            weight_y_ref[owner] = weight_y
            rows = [weight_x_ref[x, row, :] for x in range(8)]
            if by_gather:
                index = jnp.broadcast_to(element & (LANES - 1), (8, LANES))
                lower = gathered(u_ref, index, rows)
                upper = gathered(u_ref, index + 1, rows)
                along = coords_ref[2, row, :]
                totals = [low + along * (high - low) for low, high in zip(lower, upper)]
            else:
                totals = [
                    sum(
                        sums[64 * comp + 8 * x :, LANES * half : LANES * half + LANES][:8]
                        * rows[x]
                        for x in range(8)
                    )
                    for comp in range(3)
                ]
            for comp in range(3):
                places_ref[pl.ds(4 * owner + comp, 1), :] = jnp.sum(
                    totals[comp] * weight_y, axis=0, keepdims=True
                )
            places_ref[pl.ds(4 * owner + 3, 1), :] = jnp.zeros((1, LANES), F32)

    lane_block = iota((16, LANES), 1) >> 3
    pick = (lane_block == iota((16, LANES), 0)).astype(F32)
    kind = jnp.dot(
        jnp.broadcast_to(class_ref[...].astype(F32), (8, 16)), pick, preferred_element_type=F32
    )
    factor = jnp.zeros((8, LANES), F32)
    for index, value in enumerate(CLASS_VALUES):
        factor = factor + jnp.where(kind == float(index), value, 0.0)
    density = density_ref[...]
    modulus_ref[...] = factor[None] * density * density
    odd_dom, end = odd_dom_index(), at_end(DOM)
    for comp in range(5):
        source = modulus_ref if comp == 3 else density_ref if comp == 4 else u_ref.at[comp]
        first, last = source[0], source[7]
        even_ref[comp] = jnp.where(odd_dom, first, last)
        odd_ref[comp] = jnp.where(end, 0.0, jnp.where(odd_dom, last, first))
    for copy in copies[5:]:
        copy.wait()


def weights_kernel(element_ref, coords_ref, depth_ref):
    for owner in range(32):
        row = pl.ds(owner, 1)
        high, low = depth_weights(element_ref[row, :], coords_ref[2, row, :])
        depth_ref[owner, pl.ds(0, LANES), :] = high
        depth_ref[owner, pl.ds(LANES, LANES), :] = low


def fibre_tables_kernel(
    slots_ref, angles_ref, stiffness_ref, direction_ref, stiff_ref, fibre_ref, node_ref
):
    square = iota((16, 16), 0) == iota((16, 16), 1)
    stiffness = jnp.sum(jnp.where(square, stiffness_ref[...], 0.0), axis=1, keepdims=True)
    stiff_ref[...] = jnp.where(iota((16, LANES), 1) < LANES - 1, stiffness, 0.0)
    azimuth, elevation = angles_ref[0], angles_ref[1]
    flat = jnp.cos(elevation)
    direction_ref[0] = jnp.cos(azimuth) * flat
    direction_ref[1] = jnp.sin(azimuth) * flat
    direction_ref[2] = jnp.sin(elevation)
    lefts, rights = [], []
    nodes = iota((1, LANES), 1).astype(F32)
    for fibre in range(16):
        slots = slots_ref[pl.ds(fibre, 1), :]
        host = iota((32, LANES), 0) == (slots >> 7)
        lefts.append(
            jnp.concatenate(
                [jnp.where(host, float(fibre + 1), 0.0), jnp.where(host, nodes, 0.0)], axis=0
            ).astype(BF16)
        )
        rights.append((iota((LANES, LANES), 0) == (slots & 127)).astype(F32).astype(BF16))
    table = lax.dot_general(
        jnp.concatenate(lefts, axis=1),
        jnp.concatenate(rights, axis=1),
        (((1,), (1,)), ((), ())),
        preferred_element_type=F32,
    )
    table = table.astype(jnp.int32)
    fibre_ref[...] = table[:32]
    node_ref[...] = table[32:]


def lane_pick(row, index):
    return jnp.take_along_axis(jnp.broadcast_to(row, index.shape), index, axis=1)


def fibre_kernel(
    places_ref, slots_ref, direction_ref, stiff_ref, fibre_ref, node_ref, pulls_ref
):
    slots = slots_ref[...]
    host, spot = slots >> 7, slots & 127
    places = [jnp.zeros(slots.shape, F32) for _ in range(3)]
    for step in range(32):
        here = host == step
        for comp in range(3):
            picked = lane_pick(places_ref[pl.ds(4 * step + comp, 1), :], spot)
            places[comp] = jnp.where(here, picked, places[comp])
    strain = jnp.zeros(slots.shape, F32)
    for comp in range(3):
        ahead = pltpu.roll(places[comp], LANES - 1, 1)
        strain = strain + direction_ref[comp] * (ahead - places[comp])
    tension = stiff_ref[...] * jnp.maximum(strain, 0.0)
    forces = []
    for comp in range(3):
        pull = tension * direction_ref[comp]
        forces.append(pull - pltpu.roll(pull, 1, 1))
    for block in range(4):
        fibre = fibre_ref[pl.ds(8 * block, 8), :]
        node = node_ref[pl.ds(8 * block, 8), :]
        placed = [jnp.zeros((8, LANES), F32) for _ in range(3)]
        for step in range(16):
            here = fibre == step + 1
            for comp in range(3):
                picked = lane_pick(forces[comp][step : step + 1], node)
                placed[comp] = jnp.where(here, picked, placed[comp])
        for comp in range(3):
            pulls_ref[pl.ds(32 * block + comp, 8, stride=4), :] = placed[comp]
        pulls_ref[pl.ds(32 * block + 3, 8, stride=4), :] = jnp.zeros((8, LANES), F32)


def sides_kernel(
    u_ref, density_ref, modulus_ref, even_in_ref, odd_in_ref, even_ref, odd_swap_ref
):
    odd_dom = odd_dom_index()
    odd_blk, end = odd_blk_index(), at_end("blk")
    for comp in range(5):
        lower = jnp.where(odd_dom, even_in_ref[comp], odd_in_ref[comp])
        upper = jnp.where(odd_dom, odd_in_ref[comp], even_in_ref[comp])
        rows = []
        for at in (0, 7):
            if comp < 3:
                own = u_ref[comp, :, at, :]
            else:
                own = (modulus_ref if comp == 3 else density_ref)[:, at, :]
            rows.append(
                jnp.concatenate([lower[at : at + 1], own, upper[at : at + 1]], axis=0)
            )
        first, last = rows
        even_ref[pl.ds(10 * comp, 10), :] = jnp.where(odd_blk, first, last)
        odd_swap_ref[pl.ds(10 * comp, 10), :] = jnp.where(
            end, 0.0, jnp.where(odd_blk, last, first)
        )


def elastic_kernel(
    u_ref, velocity_ref, load_ref, density_ref, modulus_ref,
    even_x_ref, odd_x_ref, even_y_ref, odd_y_ref,
    velocity_out_ref, displacement_out_ref, inverse_mass_ref,
    nodes_ref, depth_ref, corner_ref,
):
    odd_dom = odd_dom_index()
    odd_blk = odd_blk_index()
    for comp in range(5):
        nodes_ref[comp, pl.ds(96, 24), :] = jnp.zeros((24, LANES), F32)
        lower = jnp.where(odd_dom, even_x_ref[comp], odd_x_ref[comp])
        upper = jnp.where(odd_dom, odd_x_ref[comp], even_x_ref[comp])
        nodes_ref[comp, pl.ds(1, 8), :] = lower
        nodes_ref[comp, pl.ds(91, 8), :] = upper
        for x in range(8):
            if comp < 3:
                own = u_ref[comp, x]
            else:
                own = (modulus_ref if comp == 3 else density_ref)[x]
            nodes_ref[comp, pl.ds(10 * x + 11, 8), :] = own
        even = even_y_ref[pl.ds(10 * comp, 10), :]
        odd = odd_y_ref[pl.ds(10 * comp, 10), :]
        left = jnp.where(odd_blk, even, odd)
        right = jnp.where(odd_blk, odd, even)
        for x in range(10):
            nodes_ref[comp, pl.ds(10 * x, 1), :] = left[x : x + 1]
            nodes_ref[comp, pl.ds(10 * x + 9, 1), :] = right[x : x + 1]
    last_lane = iota((8, LANES), 1) == LANES - 1
    first_lane = iota((8, LANES), 1) == 0
    for comp in range(3):
        for chunk in range(ROWS_PAD // 8):
            here = nodes_ref[comp, pl.ds(8 * chunk, 8), :]
            above = jnp.where(last_lane, 0.0, pltpu.roll(here, LANES - 1, 1))
            depth_ref[2 * comp, pl.ds(8 * chunk, 8), :] = above + here
            depth_ref[2 * comp + 1, pl.ds(8 * chunk, 8), :] = above - here

    long, cross, shear = (LAME + 2 * SHEAR) / 16, LAME / 16, SHEAR / 16
    long3, cross3, shear3 = (LAME + 3 * SHEAR) / 48, LAME / 48, SHEAR / 48
    long9 = (LAME + 4 * SHEAR) / 144
    for chunk in range(ROWS // 8):
        at = 8 * chunk
        mode = {}
        for comp in range(3):
            for c in range(2):
                a00 = depth_ref[2 * comp + c, pl.ds(at, 8), :]
                a01 = depth_ref[2 * comp + c, pl.ds(at + 1, 8), :]
                a10 = depth_ref[2 * comp + c, pl.ds(at + 10, 8), :]
                a11 = depth_ref[2 * comp + c, pl.ds(at + 11, 8), :]
                s0, d0, s1, d1 = a00 + a01, a01 - a00, a10 + a11, a11 - a10
                mode[comp, 0, 0, c] = s0 + s1
                mode[comp, 0, 1, c] = d0 + d1
                mode[comp, 1, 0, c] = s1 - s0
                mode[comp, 1, 1, c] = d1 - d0
        scale = nodes_ref[3, pl.ds(at, 8), :]
        u100, v010, w001 = mode[0, 1, 0, 0], mode[1, 0, 1, 0], mode[2, 0, 0, 1]
        trace = cross * (u100 + v010 + w001)
        f = {}
        f[0, 1, 0, 0] = (long - cross) * u100 + trace
        f[1, 0, 1, 0] = (long - cross) * v010 + trace
        f[2, 0, 0, 1] = (long - cross) * w001 + trace
        f[0, 0, 1, 0] = f[1, 1, 0, 0] = shear * (mode[0, 0, 1, 0] + mode[1, 1, 0, 0])
        f[0, 0, 0, 1] = f[2, 1, 0, 0] = shear * (mode[0, 0, 0, 1] + mode[2, 1, 0, 0])
        f[1, 0, 0, 1] = f[2, 0, 1, 0] = shear * (mode[1, 0, 0, 1] + mode[2, 0, 1, 0])
        for one, two in (
            ((0, 1, 1, 0), (2, 0, 1, 1)),
            ((0, 1, 0, 1), (1, 0, 1, 1)),
            ((1, 1, 1, 0), (2, 1, 0, 1)),
        ):
            f[one] = long3 * mode[one] + cross3 * mode[two]
            f[two] = long3 * mode[two] + cross3 * mode[one]
        twist = mode[0, 0, 1, 1] + mode[1, 1, 0, 1] + mode[2, 1, 1, 0]
        for key in ((0, 0, 1, 1), (1, 1, 0, 1), (2, 1, 1, 0)):
            f[key] = shear3 * (twist + mode[key])
        for comp in range(3):
            f[comp, 1, 1, 1] = long9 * mode[comp, 1, 1, 1]
        f = {key: value * scale for key, value in f.items()}
        for comp in range(3):
            for c in range(2):
                m01, m10, m11 = f[comp, 0, 1, c], f[comp, 1, 0, c], f[comp, 1, 1, c]
                total, other = m10 + m01, m10 - m01
                corners = (m11 - total, -m11 - other, other - m11, total + m11)
                if c == 1:
                    m00 = f[comp, 0, 0, 1]
                    corners = tuple(corner + m00 for corner in corners)
                for which in range(4):
                    corner_ref[8 * comp + 4 * c + which, pl.ds(at + 16, 8), :] = corners[which]

    shifts = (0, 1, 10, 11)
    for x in range(8):
        at = 10 * x + 11
        weight = sum(nodes_ref[4, pl.ds(at - shift, 8), :] for shift in shifts)
        below = jnp.where(first_lane, 0.0, pltpu.roll(weight, 1, 1))
        inverse = 1.0 / (0.125 * (weight + below))
        inverse_mass_ref[x] = inverse
        for comp in range(3):
            h0, h1 = (
                sum(
                    corner_ref[8 * comp + 4 * c + which, pl.ds(at + 16 - shift, 8), :]
                    for which, shift in enumerate(shifts)
                )
                for c in range(2)
            )
            below = jnp.where(first_lane, 0.0, pltpu.roll(h0 + h1, 1, 1))
            elastic = h0 - h1 + below
            velocity = velocity_ref[comp, x]
            acceleration = (load_ref[comp, x] - elastic) * inverse - DAMPING * velocity
            velocity = velocity + TIME_STEP * acceleration
            velocity_out_ref[comp, x] = velocity
            displacement_out_ref[comp, x] = u_ref[comp, x] + TIME_STEP * velocity


def spread_kernel(
    pulls_ref, depth_ref, weight_x_ref, weight_y_ref,
    velocity_ref, displacement_ref, inverse_mass_ref,
    displacement_out_ref, velocity_out_ref, terms_ref,
):
    for owner in range(32):
        weight_y = weight_y_ref[owner]
        planar = jnp.concatenate(
            [weight_y * weight_x_ref[x, pl.ds(owner, 1), :] for x in range(8)], axis=0
        )
        for comp in range(3):
            high, low = split(planar * pulls_ref[pl.ds(4 * owner + comp, 1), :])
            terms_ref[owner, pl.ds(64 * comp, 64), :] = high
            terms_ref[owner, pl.ds(192 + 64 * comp, 64), :] = low
    total = lax.dot_general(
        jnp.concatenate([terms_ref[owner] for owner in range(32)], axis=1),
        jnp.concatenate([depth_ref[owner] for owner in range(32)], axis=1),
        (((1,), (1,)), ((), ())),
        preferred_element_type=F32,
    )
    fibre = (total[:192, :LANES] + total[192:, :LANES]) + (
        total[:192, LANES:] + total[192:, LANES:]
    )
    for comp in range(3):
        for x in range(8):
            row = 64 * comp + 8 * x
            change = TIME_STEP * (fibre[row : row + 8] * inverse_mass_ref[x])
            velocity_out_ref[comp, x] = velocity_ref[comp, x] + change
            displacement_out_ref[comp, x] = displacement_ref[comp, x] + TIME_STEP * change


VMEM = pl.BlockSpec(memory_space=pltpu.VMEM)


def call(kernel, outs, ins, scratch=(), final=False, first=False):
    space = jax.ShapeDtypeStruct if final else pltpu.VMEM
    outs = tuple(space(shape, dtype) for shape, dtype in outs)
    space_in = pltpu.HBM if first else pltpu.VMEM
    ins = tuple(pltpu.with_memory_space_constraint(value, space_in) for value in ins)
    return pl.pallas_call(
        kernel,
        out_shape=outs,
        in_specs=[pl.BlockSpec(memory_space=space_in)] * len(ins),
        out_specs=(VMEM,) * len(outs),
        scratch_shapes=scratch,
        compiler_params=pltpu.CompilerParams(vmem_limit_bytes=16 << 20),
    )(*ins)


def swap(shard, axis, first):
    doms = lax.axis_size(DOM)
    blks = lax.axis_size("blk")
    pairs = []
    for dom in range(doms):
        for blk in range(blks):
            at, size = (blk, blks) if axis == "blk" else (dom, doms)
            low = (at - first) % 2 == 0
            move = 1 if low else -1
            along_blk = (axis == "blk") == (0 <= at + move < size)
            if not 0 <= at + move < size:
                move = 1 if (dom if axis == "blk" else blk) % 2 == 0 else -1
            target = (dom, blk + move) if along_blk else (dom + move, blk)
            pairs.append((dom * blks + blk, target[0] * blks + target[1]))
    return lax.ppermute(shard, (*DOM, "blk"), pairs)


def exchange(rows):
    blocks = rows.reshape(32, 4, LANES)
    blocks = lax.all_to_all(blocks, DOM, split_axis=0, concat_axis=0, tiled=True)
    return blocks.reshape(128, LANES)


def step(
    displacement, velocity, load, density, block_class,
    host_element, host_coords, fibre_slot, fibre_angles, fibre_stiffness,
):
    grid = (3, 8, 8, LANES)
    plane = (8, 8, LANES)
    side = ((50, LANES), F32)
    arguments = (
        displacement,
        host_element.reshape(32, LANES),
        host_coords.reshape(3, 32, LANES),
        density,
        block_class.reshape(1, 16),
        velocity,
        load,
        fibre_slot.reshape(16, LANES),
        fibre_angles.reshape(2, 16, LANES),
        fibre_stiffness.reshape(1, 16),
    )
    places, modulus, even_x, odd_x, weight_x, weight_y, *arguments = call(
        interpolate_kernel,
        (
            ((128, LANES), F32), (plane, F32), ((5, 8, LANES), F32), ((5, 8, LANES), F32),
            ((8, 32, LANES), F32), ((32, 8, LANES), F32),
        )
        + tuple((value.shape, value.dtype) for value in arguments),
        arguments,
        scratch=(pltpu.SemaphoreType.DMA((len(arguments),)),),
        first=True,
    )
    displacement, element, coords, density, _, velocity, load, slots, angles, stiffness = arguments
    even_x = swap(even_x, DOM, 0)
    odd_x = swap(odd_x, DOM, 1)
    received = exchange(places)
    table = ((32, LANES), jnp.int32)
    direction, stiff, fibre, node = call(
        fibre_tables_kernel,
        (((3, 16, LANES), F32), ((16, LANES), F32), table, table),
        (slots, angles, stiffness),
    )
    even_y, odd_y = call(
        sides_kernel, (side, side), (displacement, density, modulus, even_x, odd_x)
    )
    even_y = swap(even_y, "blk", 0)
    odd_y = swap(odd_y, "blk", 1)
    (pulls,) = call(
        fibre_kernel, (((128, LANES), F32),),
        (received, slots, direction, stiff, fibre, node),
    )
    returned = exchange(pulls)
    (depth,) = call(weights_kernel, (((32, 256, LANES), BF16),), (element, coords))
    new_velocity, new_displacement, inverse_mass = call(
        elastic_kernel,
        ((grid, F32), (grid, F32), (plane, F32)),
        (
            displacement, velocity, load, density, modulus,
            even_x, odd_x, even_y, odd_y,
        ),
        scratch=(
            pltpu.VMEM((5, ROWS_PAD, LANES), F32),
            pltpu.VMEM((6, ROWS_PAD, LANES), F32),
            pltpu.VMEM((24, ROWS_PAD, LANES), F32),
        ),
    )
    return call(
        spread_kernel, ((grid, F32), (grid, F32)),
        (returned, depth, weight_x, weight_y, new_velocity, new_displacement, inverse_mass),
        scratch=(pltpu.VMEM((32, 384, LANES), BF16),),
        final=True,
    )


def solution(mesh):
    finer = Mesh(
        mesh.devices.reshape(4, 4, 2, mesh.shape["blk"]), ("dom_0", "dom_1", "dom_2", "blk")
    )
    in_specs = (
        P(None, DOM, "blk", None),
        P(None, DOM, "blk", None),
        P(None, DOM, "blk", None),
        P(DOM, "blk", None),
        P(DOM, "blk", None),
        P("blk", DOM),
        P(None, "blk", DOM),
        P(DOM, "blk", None),
        P(None, DOM, "blk", None),
        P(DOM, "blk"),
    )
    out_specs = (P(None, DOM, "blk", None), P(None, DOM, "blk", None))
    return jax.shard_map(step, mesh=finer, in_specs=in_specs, out_specs=out_specs, check_vma=False)
```

```python
import jax
import jax.numpy as jnp
from jax import lax
from jax.experimental import pallas as pl
from jax.experimental.pallas import tpu as pltpu
from jax.sharding import Mesh
from jax.sharding import PartitionSpec as P

DOM = ("dom_0", "dom_1", "dom_2")
CLASS_VALUES = (1.0, 0.45, 0.12)
TIME_STEP = 0.25
DAMPING = 0.5
LAME = 0.3 / (1.3 * 0.4)
SHEAR = 0.5 / 1.3

F32 = jnp.float32
BF16 = jnp.bfloat16
LANES = 128
GATHERED = (2, 5, 8, 11, 14)
ROWS = 104
ROWS_PAD = 120


def odd_dom_index():
    return lax.axis_index("dom_2") == 1


def odd_blk_index():
    return (lax.axis_index("blk") & 1) == 1


def at_end(axis):
    axes = axis if isinstance(axis, tuple) else (axis,)
    index, size = 0, 1
    for name in axes:
        index = index * lax.axis_size(name) + lax.axis_index(name)
        size *= lax.axis_size(name)
    return (index == 0) | (index == size - 1)


def split(value):
    high = value.astype(BF16)
    low = (value - high.astype(F32)).astype(BF16)
    return high, low


def iota(shape, axis):
    return lax.broadcasted_iota(jnp.int32, shape, axis)


def hat(lowest, along, count):
    where = iota((count, LANES), 0)
    return jnp.where(
        where == lowest, 1.0 - along, jnp.where(where == lowest + 1, along, 0.0)
    )


def depth_weights(element, along):
    shape = (LANES, LANES)
    lowest = jnp.broadcast_to(element & (LANES - 1), shape).astype(jnp.int16)
    where = lax.broadcasted_iota(jnp.int16, shape, 0)
    here, above = where == lowest, where == lowest + jnp.int16(1)
    zero = jnp.zeros(shape, BF16)
    parts = []
    for lower, upper in zip(split(1.0 - along), split(along)):
        lower = jnp.broadcast_to(lower.astype(F32), shape).astype(BF16)
        upper = jnp.broadcast_to(upper.astype(F32), shape).astype(BF16)
        parts.append(jnp.where(here, lower, jnp.where(above, upper, zero)))
    return parts


def gathered(field_ref, index, rows):
    return [
        sum(
            jnp.take_along_axis(field_ref[comp, x], index, axis=1) * rows[x] for x in range(8)
        )
        for comp in range(3)
    ]


def interpolate_kernel(*refs):
    count = (len(refs) - 4) // 2
    sources, targets, semaphores = refs[:count], refs[count + 3 : -1], refs[-1]
    places_ref, weight_x_ref, weight_y_ref = refs[count : count + 3]
    copies = [
        pltpu.make_async_copy(source, target, semaphores.at[index])
        for index, (source, target) in enumerate(zip(sources, targets))
    ]
    for copy in copies:
        copy.start()
    u_ref, element_ref, coords_ref = targets[:3]
    for copy in copies[:3]:
        copy.wait()
    lowest, along = element_ref[...] >> 10, coords_ref[0]
    for x in range(8):
        weight_x_ref[x] = jnp.where(
            lowest == x, 1.0 - along, jnp.where(lowest == x - 1, along, 0.0)
        )
    field_high, field_low = split(u_ref[...].reshape(192, LANES))
    field = jnp.concatenate([field_high, field_low, field_high], axis=1)
    for pair in range(16):
        by_gather = pair in GATHERED
        if not by_gather:
            parts = []
            for owner in (2 * pair, 2 * pair + 1):
                row = pl.ds(owner, 1)
                high, low = depth_weights(element_ref[row, :], coords_ref[2, row, :])
                parts.append(jnp.concatenate([high, high, low], axis=0))
            sums = jnp.dot(field, jnp.concatenate(parts, axis=1), preferred_element_type=F32)
        for half in range(2):
            owner = 2 * pair + half
            row = pl.ds(owner, 1)
            element = element_ref[row, :]
            weight_y = hat((element >> 7) & 7, coords_ref[1, row, :], 8)
            weight_y_ref[owner] = weight_y
            rows = [weight_x_ref[x, row, :] for x in range(8)]
            if by_gather:
                index = jnp.broadcast_to(element & (LANES - 1), (8, LANES))
                lower = gathered(u_ref, index, rows)
                upper = gathered(u_ref, index + 1, rows)
                along = coords_ref[2, row, :]
                totals = [low + along * (high - low) for low, high in zip(lower, upper)]
            else:
                totals = [
                    sum(
                        sums[64 * comp + 8 * x :, LANES * half : LANES * half + LANES][:8]
                        * rows[x]
                        for x in range(8)
                    )
                    for comp in range(3)
                ]
            for comp in range(3):
                places_ref[pl.ds(4 * owner + comp, 1), :] = jnp.sum(
                    totals[comp] * weight_y, axis=0, keepdims=True
                )
            places_ref[pl.ds(4 * owner + 3, 1), :] = jnp.zeros((1, LANES), F32)

    for copy in copies[3:]:
        copy.wait()


def rows_kernel(u_ref, density_ref, class_ref, modulus_ref, even_ref, odd_ref):
    lane_block = iota((16, LANES), 1) >> 3
    pick = (lane_block == iota((16, LANES), 0)).astype(F32)
    kind = jnp.dot(
        jnp.broadcast_to(class_ref[...].astype(F32), (8, 16)), pick, preferred_element_type=F32
    )
    factor = jnp.zeros((8, LANES), F32)
    for index, value in enumerate(CLASS_VALUES):
        factor = factor + jnp.where(kind == float(index), value, 0.0)
    density = density_ref[...]
    modulus_ref[...] = factor[None] * density * density
    odd_dom, end = odd_dom_index(), at_end(DOM)
    for comp in range(5):
        source = modulus_ref if comp == 3 else density_ref if comp == 4 else u_ref.at[comp]
        first, last = source[0], source[7]
        even_ref[comp] = jnp.where(odd_dom, first, last)
        odd_ref[comp] = jnp.where(end, 0.0, jnp.where(odd_dom, last, first))


def weights_kernel(element_ref, coords_ref, depth_ref):
    for owner in range(32):
        row = pl.ds(owner, 1)
        high, low = depth_weights(element_ref[row, :], coords_ref[2, row, :])
        depth_ref[owner, pl.ds(0, LANES), :] = high
        depth_ref[owner, pl.ds(LANES, LANES), :] = low


def fibre_tables_kernel(
    slots_ref, angles_ref, stiffness_ref, direction_ref, stiff_ref, fibre_ref, node_ref
):
    square = iota((16, 16), 0) == iota((16, 16), 1)
    stiffness = jnp.sum(jnp.where(square, stiffness_ref[...], 0.0), axis=1, keepdims=True)
    stiff_ref[...] = jnp.where(iota((16, LANES), 1) < LANES - 1, stiffness, 0.0)
    azimuth, elevation = angles_ref[0], angles_ref[1]
    flat = jnp.cos(elevation)
    direction_ref[0] = jnp.cos(azimuth) * flat
    direction_ref[1] = jnp.sin(azimuth) * flat
    direction_ref[2] = jnp.sin(elevation)
    lefts, rights = [], []
    nodes = iota((1, LANES), 1).astype(F32)
    for fibre in range(16):
        slots = slots_ref[pl.ds(fibre, 1), :]
        host = iota((32, LANES), 0) == (slots >> 7)
        lefts.append(
            jnp.concatenate(
                [jnp.where(host, float(fibre + 1), 0.0), jnp.where(host, nodes, 0.0)], axis=0
            ).astype(BF16)
        )
        rights.append((iota((LANES, LANES), 0) == (slots & 127)).astype(F32).astype(BF16))
    table = lax.dot_general(
        jnp.concatenate(lefts, axis=1),
        jnp.concatenate(rights, axis=1),
        (((1,), (1,)), ((), ())),
        preferred_element_type=F32,
    )
    table = table.astype(jnp.int32)
    fibre_ref[...] = table[:32]
    node_ref[...] = table[32:]


def lane_pick(row, index):
    return jnp.take_along_axis(jnp.broadcast_to(row, index.shape), index, axis=1)


def fibre_kernel(
    places_ref, slots_ref, direction_ref, stiff_ref, fibre_ref, node_ref, pulls_ref
):
    slots = slots_ref[...]
    host, spot = slots >> 7, slots & 127
    places = [jnp.zeros(slots.shape, F32) for _ in range(3)]
    for step in range(32):
        here = host == step
        for comp in range(3):
            picked = lane_pick(places_ref[pl.ds(4 * step + comp, 1), :], spot)
            places[comp] = jnp.where(here, picked, places[comp])
    strain = jnp.zeros(slots.shape, F32)
    for comp in range(3):
        ahead = pltpu.roll(places[comp], LANES - 1, 1)
        strain = strain + direction_ref[comp] * (ahead - places[comp])
    tension = stiff_ref[...] * jnp.maximum(strain, 0.0)
    forces = []
    for comp in range(3):
        pull = tension * direction_ref[comp]
        forces.append(pull - pltpu.roll(pull, 1, 1))
    for block in range(4):
        fibre = fibre_ref[pl.ds(8 * block, 8), :]
        node = node_ref[pl.ds(8 * block, 8), :]
        placed = [jnp.zeros((8, LANES), F32) for _ in range(3)]
        for step in range(16):
            here = fibre == step + 1
            for comp in range(3):
                picked = lane_pick(forces[comp][step : step + 1], node)
                placed[comp] = jnp.where(here, picked, placed[comp])
        for comp in range(3):
            pulls_ref[pl.ds(32 * block + comp, 8, stride=4), :] = placed[comp]
        pulls_ref[pl.ds(32 * block + 3, 8, stride=4), :] = jnp.zeros((8, LANES), F32)


def sides_kernel(
    u_ref, density_ref, modulus_ref, even_in_ref, odd_in_ref, even_ref, odd_swap_ref
):
    odd_dom = odd_dom_index()
    odd_blk, end = odd_blk_index(), at_end("blk")
    for comp in range(5):
        lower = jnp.where(odd_dom, even_in_ref[comp], odd_in_ref[comp])
        upper = jnp.where(odd_dom, odd_in_ref[comp], even_in_ref[comp])
        rows = []
        for at in (0, 7):
            if comp < 3:
                own = u_ref[comp, :, at, :]
            else:
                own = (modulus_ref if comp == 3 else density_ref)[:, at, :]
            rows.append(
                jnp.concatenate([lower[at : at + 1], own, upper[at : at + 1]], axis=0)
            )
        first, last = rows
        even_ref[pl.ds(10 * comp, 10), :] = jnp.where(odd_blk, first, last)
        odd_swap_ref[pl.ds(10 * comp, 10), :] = jnp.where(
            end, 0.0, jnp.where(odd_blk, last, first)
        )


def elastic_kernel(
    u_ref, velocity_ref, load_ref, density_ref, modulus_ref,
    even_x_ref, odd_x_ref, even_y_ref, odd_y_ref,
    velocity_out_ref, displacement_out_ref, inverse_mass_ref,
    nodes_ref, depth_ref, corner_ref,
):
    odd_dom = odd_dom_index()
    odd_blk = odd_blk_index()
    for comp in range(5):
        nodes_ref[comp, pl.ds(96, 24), :] = jnp.zeros((24, LANES), F32)
        lower = jnp.where(odd_dom, even_x_ref[comp], odd_x_ref[comp])
        upper = jnp.where(odd_dom, odd_x_ref[comp], even_x_ref[comp])
        nodes_ref[comp, pl.ds(1, 8), :] = lower
        nodes_ref[comp, pl.ds(91, 8), :] = upper
        for x in range(8):
            if comp < 3:
                own = u_ref[comp, x]
            else:
                own = (modulus_ref if comp == 3 else density_ref)[x]
            nodes_ref[comp, pl.ds(10 * x + 11, 8), :] = own
        even = even_y_ref[pl.ds(10 * comp, 10), :]
        odd = odd_y_ref[pl.ds(10 * comp, 10), :]
        left = jnp.where(odd_blk, even, odd)
        right = jnp.where(odd_blk, odd, even)
        for x in range(10):
            nodes_ref[comp, pl.ds(10 * x, 1), :] = left[x : x + 1]
            nodes_ref[comp, pl.ds(10 * x + 9, 1), :] = right[x : x + 1]
    last_lane = iota((8, LANES), 1) == LANES - 1
    first_lane = iota((8, LANES), 1) == 0
    for comp in range(3):
        for chunk in range(ROWS_PAD // 8):
            here = nodes_ref[comp, pl.ds(8 * chunk, 8), :]
            above = jnp.where(last_lane, 0.0, pltpu.roll(here, LANES - 1, 1))
            depth_ref[2 * comp, pl.ds(8 * chunk, 8), :] = above + here
            depth_ref[2 * comp + 1, pl.ds(8 * chunk, 8), :] = above - here

    long, cross, shear = (LAME + 2 * SHEAR) / 16, LAME / 16, SHEAR / 16
    long3, cross3, shear3 = (LAME + 3 * SHEAR) / 48, LAME / 48, SHEAR / 48
    long9 = (LAME + 4 * SHEAR) / 144
    for chunk in range(ROWS // 8):
        at = 8 * chunk
        mode = {}
        for comp in range(3):
            for c in range(2):
                a00 = depth_ref[2 * comp + c, pl.ds(at, 8), :]
                a01 = depth_ref[2 * comp + c, pl.ds(at + 1, 8), :]
                a10 = depth_ref[2 * comp + c, pl.ds(at + 10, 8), :]
                a11 = depth_ref[2 * comp + c, pl.ds(at + 11, 8), :]
                s0, d0, s1, d1 = a00 + a01, a01 - a00, a10 + a11, a11 - a10
                mode[comp, 0, 0, c] = s0 + s1
                mode[comp, 0, 1, c] = d0 + d1
                mode[comp, 1, 0, c] = s1 - s0
                mode[comp, 1, 1, c] = d1 - d0
        scale = nodes_ref[3, pl.ds(at, 8), :]
        u100, v010, w001 = mode[0, 1, 0, 0], mode[1, 0, 1, 0], mode[2, 0, 0, 1]
        trace = cross * (u100 + v010 + w001)
        f = {}
        f[0, 1, 0, 0] = (long - cross) * u100 + trace
        f[1, 0, 1, 0] = (long - cross) * v010 + trace
        f[2, 0, 0, 1] = (long - cross) * w001 + trace
        f[0, 0, 1, 0] = f[1, 1, 0, 0] = shear * (mode[0, 0, 1, 0] + mode[1, 1, 0, 0])
        f[0, 0, 0, 1] = f[2, 1, 0, 0] = shear * (mode[0, 0, 0, 1] + mode[2, 1, 0, 0])
        f[1, 0, 0, 1] = f[2, 0, 1, 0] = shear * (mode[1, 0, 0, 1] + mode[2, 0, 1, 0])
        for one, two in (
            ((0, 1, 1, 0), (2, 0, 1, 1)),
            ((0, 1, 0, 1), (1, 0, 1, 1)),
            ((1, 1, 1, 0), (2, 1, 0, 1)),
        ):
            f[one] = long3 * mode[one] + cross3 * mode[two]
            f[two] = long3 * mode[two] + cross3 * mode[one]
        twist = mode[0, 0, 1, 1] + mode[1, 1, 0, 1] + mode[2, 1, 1, 0]
        for key in ((0, 0, 1, 1), (1, 1, 0, 1), (2, 1, 1, 0)):
            f[key] = shear3 * (twist + mode[key])
        for comp in range(3):
            f[comp, 1, 1, 1] = long9 * mode[comp, 1, 1, 1]
        f = {key: value * scale for key, value in f.items()}
        for comp in range(3):
            for c in range(2):
                m01, m10, m11 = f[comp, 0, 1, c], f[comp, 1, 0, c], f[comp, 1, 1, c]
                total, other = m10 + m01, m10 - m01
                corners = (m11 - total, -m11 - other, other - m11, total + m11)
                if c == 1:
                    m00 = f[comp, 0, 0, 1]
                    corners = tuple(corner + m00 for corner in corners)
                for which in range(4):
                    corner_ref[8 * comp + 4 * c + which, pl.ds(at + 16, 8), :] = corners[which]

    shifts = (0, 1, 10, 11)
    for x in range(8):
        at = 10 * x + 11
        weight = sum(nodes_ref[4, pl.ds(at - shift, 8), :] for shift in shifts)
        below = jnp.where(first_lane, 0.0, pltpu.roll(weight, 1, 1))
        inverse = 1.0 / (0.125 * (weight + below))
        inverse_mass_ref[x] = inverse
        for comp in range(3):
            h0, h1 = (
                sum(
                    corner_ref[8 * comp + 4 * c + which, pl.ds(at + 16 - shift, 8), :]
                    for which, shift in enumerate(shifts)
                )
                for c in range(2)
            )
            below = jnp.where(first_lane, 0.0, pltpu.roll(h0 + h1, 1, 1))
            elastic = h0 - h1 + below
            velocity = velocity_ref[comp, x]
            acceleration = (load_ref[comp, x] - elastic) * inverse - DAMPING * velocity
            velocity = velocity + TIME_STEP * acceleration
            velocity_out_ref[comp, x] = velocity
            displacement_out_ref[comp, x] = u_ref[comp, x] + TIME_STEP * velocity


def spread_kernel(
    pulls_ref, depth_ref, weight_x_ref, weight_y_ref,
    velocity_ref, displacement_ref, inverse_mass_ref,
    displacement_out_ref, velocity_out_ref, terms_ref,
):
    for owner in range(32):
        weight_y = weight_y_ref[owner]
        planar = jnp.concatenate(
            [weight_y * weight_x_ref[x, pl.ds(owner, 1), :] for x in range(8)], axis=0
        )
        for comp in range(3):
            high, low = split(planar * pulls_ref[pl.ds(4 * owner + comp, 1), :])
            terms_ref[owner, pl.ds(64 * comp, 64), :] = high
            terms_ref[owner, pl.ds(192 + 64 * comp, 64), :] = low
    total = lax.dot_general(
        jnp.concatenate([terms_ref[owner] for owner in range(32)], axis=1),
        jnp.concatenate([depth_ref[owner] for owner in range(32)], axis=1),
        (((1,), (1,)), ((), ())),
        preferred_element_type=F32,
    )
    fibre = (total[:192, :LANES] + total[192:, :LANES]) + (
        total[:192, LANES:] + total[192:, LANES:]
    )
    for comp in range(3):
        for x in range(8):
            row = 64 * comp + 8 * x
            change = TIME_STEP * (fibre[row : row + 8] * inverse_mass_ref[x])
            velocity_out_ref[comp, x] = velocity_ref[comp, x] + change
            displacement_out_ref[comp, x] = displacement_ref[comp, x] + TIME_STEP * change


VMEM = pl.BlockSpec(memory_space=pltpu.VMEM)


def call(kernel, outs, ins, scratch=(), final=False, first=False):
    space = jax.ShapeDtypeStruct if final else pltpu.VMEM
    outs = tuple(space(shape, dtype) for shape, dtype in outs)
    space_in = pltpu.HBM if first else pltpu.VMEM
    ins = tuple(pltpu.with_memory_space_constraint(value, space_in) for value in ins)
    return pl.pallas_call(
        kernel,
        out_shape=outs,
        in_specs=[pl.BlockSpec(memory_space=space_in)] * len(ins),
        out_specs=(VMEM,) * len(outs),
        scratch_shapes=scratch,
        compiler_params=pltpu.CompilerParams(vmem_limit_bytes=16 << 20),
    )(*ins)


def swap(shard, axis, first):
    doms = lax.axis_size(DOM)
    blks = lax.axis_size("blk")
    pairs = []
    for dom in range(doms):
        for blk in range(blks):
            at, size = (blk, blks) if axis == "blk" else (dom, doms)
            low = (at - first) % 2 == 0
            move = 1 if low else -1
            along_blk = (axis == "blk") == (0 <= at + move < size)
            if not 0 <= at + move < size:
                move = 1 if (dom if axis == "blk" else blk) % 2 == 0 else -1
            target = (dom, blk + move) if along_blk else (dom + move, blk)
            pairs.append((dom * blks + blk, target[0] * blks + target[1]))
    return lax.ppermute(shard, (*DOM, "blk"), pairs)


def exchange(rows):
    blocks = rows.reshape(32, 4, LANES)
    blocks = lax.all_to_all(blocks, DOM, split_axis=0, concat_axis=0, tiled=True)
    return blocks.reshape(128, LANES)


def step(
    displacement, velocity, load, density, block_class,
    host_element, host_coords, fibre_slot, fibre_angles, fibre_stiffness,
):
    grid = (3, 8, 8, LANES)
    plane = (8, 8, LANES)
    side = ((50, LANES), F32)
    arguments = (
        displacement,
        host_element.reshape(32, LANES),
        host_coords.reshape(3, 32, LANES),
        density,
        block_class.reshape(1, 16),
        velocity,
        load,
        fibre_slot.reshape(16, LANES),
        fibre_angles.reshape(2, 16, LANES),
        fibre_stiffness.reshape(1, 16),
    )
    places, weight_x, weight_y, *arguments = call(
        interpolate_kernel,
        (((128, LANES), F32), ((8, 32, LANES), F32), ((32, 8, LANES), F32))
        + tuple((value.shape, value.dtype) for value in arguments),
        arguments,
        scratch=(pltpu.SemaphoreType.DMA((len(arguments),)),),
        first=True,
    )
    displacement, element, coords, density, kinds, velocity, load, slots, angles, stiffness = arguments
    modulus, even_x, odd_x = call(
        rows_kernel, ((plane, F32), ((5, 8, LANES), F32), ((5, 8, LANES), F32)),
        (displacement, density, kinds),
    )
    even_x = swap(even_x, DOM, 0)
    odd_x = swap(odd_x, DOM, 1)
    received = exchange(places)
    table = ((32, LANES), jnp.int32)
    direction, stiff, fibre, node = call(
        fibre_tables_kernel,
        (((3, 16, LANES), F32), ((16, LANES), F32), table, table),
        (slots, angles, stiffness),
    )
    even_y, odd_y = call(
        sides_kernel, (side, side), (displacement, density, modulus, even_x, odd_x)
    )
    even_y = swap(even_y, "blk", 0)
    odd_y = swap(odd_y, "blk", 1)
    (pulls,) = call(
        fibre_kernel, (((128, LANES), F32),),
        (received, slots, direction, stiff, fibre, node),
    )
    returned = exchange(pulls)
    (depth,) = call(weights_kernel, (((32, 256, LANES), BF16),), (element, coords))
    new_velocity, new_displacement, inverse_mass = call(
        elastic_kernel,
        ((grid, F32), (grid, F32), (plane, F32)),
        (
            displacement, velocity, load, density, modulus,
            even_x, odd_x, even_y, odd_y,
        ),
        scratch=(
            pltpu.VMEM((5, ROWS_PAD, LANES), F32),
            pltpu.VMEM((6, ROWS_PAD, LANES), F32),
            pltpu.VMEM((24, ROWS_PAD, LANES), F32),
        ),
    )
    return call(
        spread_kernel, ((grid, F32), (grid, F32)),
        (returned, depth, weight_x, weight_y, new_velocity, new_displacement, inverse_mass),
        scratch=(pltpu.VMEM((32, 384, LANES), BF16),),
        final=True,
    )


def solution(mesh):
    finer = Mesh(
        mesh.devices.reshape(4, 4, 2, mesh.shape["blk"]), ("dom_0", "dom_1", "dom_2", "blk")
    )
    in_specs = (
        P(None, DOM, "blk", None),
        P(None, DOM, "blk", None),
        P(None, DOM, "blk", None),
        P(DOM, "blk", None),
        P(DOM, "blk", None),
        P("blk", DOM),
        P(None, "blk", DOM),
        P(DOM, "blk", None),
        P(None, DOM, "blk", None),
        P(DOM, "blk"),
    )
    out_specs = (P(None, DOM, "blk", None), P(None, DOM, "blk", None))
    return jax.shard_map(step, mesh=finer, in_specs=in_specs, out_specs=out_specs, check_vma=False)
```
